1024 devices in a mesh: seq: 32 (over z), head: 4 (over x), exp: 8 (over y, core).
Axes of the slice: x: 4, y: 4, z: 32, core: 2. Of those that a mesh axis runs over, the one named last changes fastest.
Arguments:
- x_in: bfloat16 [32768, 4096], P(('seq', 'exp'), 'head'), may hold values from -6 to 6
- z_in: bfloat16 [32768, 4096], P(('seq', 'exp'), 'head'), may hold values from -6 to 6
- b_in: bfloat16 [32768, 1024], P(('seq', 'exp'), 'head'), may hold values from -1.796875 to 1.796875
- c_in: bfloat16 [32768, 1024], P(('seq', 'exp'), 'head'), may hold values from -1.796875 to 1.796875
- dt_in: float32 [32768, 64], P(('seq', 'exp'), 'head'), may hold values from -5.4 to -1.7
- a_log: float32 [64], P('head'), may hold values from -12 to 2
- d_skip: float32 [64], P('head'), may hold values from 0.5 to 2
- norm_w: float32 [4096], P('head'), may hold values from 0.5 to 1.5
- w_out: bfloat16 [4096, 1344], P('head'), may hold values from -0.09375 to 0.09375
- resid: bfloat16 [256, 128, 1344], P(('seq', 'exp'), 'head'), may hold values from -30 to 30
- routes: int32 [256, 128, 6], P(('seq', 'exp'), 'head'), may hold values from 0 to 31, all different within a row; in each aligned block of 32 rows (0 to 31, 32 to 63, ..., all dimensions but the last counted through in order) at most 16 rows name the same one
- gates: float32 [256, 128, 6], P(('seq', 'exp'), 'head'), may hold values from 0.1 to 0.7
- moe_gain: float32 [1344], replicated, may hold values from 0.5 to 1.5
- w_up: bfloat16 [32, 1344, 928], P(('head', 'exp')), may hold values from -0.15625 to 0.15625
- w_down: bfloat16 [32, 928, 1344], P(('head', 'exp')), may hold values from -0.1875 to 0.1875
Outputs:
- output: bfloat16 [256, 128, 1344], P(('seq', 'exp'), 'head')
The draws below stay inside these ranges and needn't reach their ends.
Inputs may be any that keep to these rules, and one draw needn't show every extreme that they name: `routes`: within the 32 aligned rows of one device no expert is named more than 16 times, and in every draw some expert is named exactly 16 times within some device's rows.
All inputs are finite; a program needn't handle non-finite values.
Results may differ from the reference program's by a relative error of at most 0.018.
Values may be sent and summed in bfloat16 or wider, within the bound.
A program may use at most 64 MiB of HBM per device.

```python
import math
import jax
import jax.numpy as jnp
import numpy as np
from jax import lax

D = 1344
HEADS = 64
HEAD_DIM = 64
STATE = 128
GROUPS = 8
STRETCH = 128
FFW = 928
TOPK = 6
TOK_DEV = 128
SHARDS = 256
TOKENS = 32768
INNER = 4096
ROWS_MOE = 32
EXPERTS = 32
CAP = 16


def draw_dt_in(key, part):
    subkeys = jax.random.split(jax.random.fold_in(key, 11), 4)
    blocks = TOKENS // TOK_DEV
    base_values = jax.random.uniform(subkeys[0], (blocks, TOK_DEV, HEADS), jnp.float32, -3.6, -2.6)
    coin = jax.random.uniform(subkeys[1], (blocks, 1, HEADS), jnp.float32)
    high_offset = jax.random.uniform(subkeys[2], (blocks, 1, HEADS), jnp.float32, 0.4, 0.9)
    low_offset = jax.random.uniform(subkeys[3], (blocks, 1, HEADS), jnp.float32, -1.8, -1.2)
    offset = jnp.where(coin < 0.5, high_offset, low_offset)
    return (base_values + offset).reshape(TOKENS, HEADS)


def draw_a_log(key, part):
    subkeys = jax.random.split(jax.random.fold_in(key, 23), 4)
    choose = jax.random.uniform(subkeys[0], (HEADS,), jnp.float32)
    quick = jnp.log(jax.random.uniform(subkeys[1], (HEADS,), jnp.float32, 0.45, 0.75))
    lasting = jnp.log(jax.random.uniform(subkeys[2], (HEADS,), jnp.float32, 0.7, 2.3) / (0.045 * TOKENS))
    between = lasting + jax.random.uniform(subkeys[3], (HEADS,), jnp.float32) * (quick - lasting)
    return jnp.where(choose < 0.4, quick, jnp.where(choose < 0.8, lasting, between))


def draw_resid(key, part):
    subkeys = jax.random.split(jax.random.fold_in(key, 37), 3)
    full_shape = (SHARDS, TOK_DEV, D)
    row_scale = jnp.exp(jax.random.uniform(subkeys[1], (SHARDS, TOK_DEV, 1), jnp.float32, jnp.log(0.2), jnp.log(2.0)))
    col_scale = jnp.exp(jax.random.uniform(subkeys[2], (1, 1, D), jnp.float32, jnp.log(0.3), jnp.log(3.0)))
    values = jnp.clip(jax.random.normal(subkeys[0], full_shape, jnp.float32), -3.0, 3.0)
    return (values * row_scale * col_scale).astype(jnp.bfloat16)


def block_levels(key, shape, cuts, least, top_value):
    level = 1.0
    for axis_at, blocks in cuts:
        draws = jax.random.uniform(jax.random.fold_in(jax.random.fold_in(key, 6), axis_at), (blocks,), jnp.float32, least / len(cuts), top_value / len(cuts))
        level = level * jnp.repeat(jnp.exp(draws), shape[axis_at] // blocks).reshape((-1,) + (1,) * (len(shape) - 1 - axis_at))
    return level


def deal_out(key, own, number, rows, amount, top, bound, slope):
    ranking = jax.random.permutation(key, amount)
    packed, ordinary = portions_of(amount, rows * top, bound, slope, True), portions_of(amount, rows * top, bound, slope, False)
    places = jnp.arange(amount)

    def named(sizes, offset_by):
        used = int((sizes > 0).sum())
        fixed = max(1, used // 4)
        shifted = fixed + (places - fixed + offset_by * (used - fixed)) % max(1, amount - fixed)
        return jnp.zeros((amount,), jnp.int32).at[ranking[jnp.where(places < fixed, places, shifted)]].set(jnp.asarray(sizes, jnp.int32))

    sizes = jnp.where(number % 4 == 0, named(packed, number // 4), named(ordinary, number - number // 4 - 1))
    mixed = jax.random.permutation(jax.random.fold_in(own, 3), amount)
    source_of, receiver = mixed[0:amount // 2 * 2:2], mixed[1:amount // 2 * 2:2]
    room = jnp.minimum(sizes[source_of] - 1, bound - sizes[receiver]) // 2
    room = jnp.where((source_of == ranking[0]) | (receiver == ranking[0]) | (sizes[receiver] == 0), 0, jnp.maximum(room, 0))
    shifted = jax.random.randint(jax.random.fold_in(own, 4), (amount // 2,), 0, 1 << 20) % (room + 1)
    sizes = sizes.at[source_of].add(-shifted).at[receiver].add(shifted)
    items = jnp.searchsorted(jnp.cumsum(sizes), jnp.arange(rows * top), side="right").astype(jnp.int32)
    table = items.reshape(top, rows).T
    table = table[jax.random.permutation(jax.random.fold_in(own, 1), rows)]
    offset_by = jax.random.randint(jax.random.fold_in(own, 2), (rows, 1), 0, top)
    return jnp.take_along_axis(table, (jnp.arange(top)[None, :] + offset_by) % top, axis=1)


def portions_of(count, total, bound, lean, full):
    loads = [(1 << 20) // math.isqrt(rank ** lean) + 1 for rank in range(1, count + 1)]
    largest = bound if full else min(bound, max(-(-total // count), total * loads[0] // sum(loads)))
    least = 1 if total - largest >= count - 1 else 0
    counts, rest = [largest] + [least] * (count - 1), total - largest - least * (count - 1)
    while rest > 0:
        movable = [i for i in range(1, count) if counts[i] < largest] or [i for i in range(1, count) if counts[i] < bound]
        whole, remaining = sum([loads[i] for i in movable]), rest
        for i in movable:
            addition = min(bound - counts[i], max(1, remaining * loads[i] // whole), rest)
            counts[i] = counts[i] + addition
            rest = rest - addition
    return np.array(counts)


def noise(key, extent, spread, reach, cuts=(), held_as=jnp.bfloat16):
    drawn = jax.random.normal(key, extent, jnp.float32) * spread
    if len(cuts) > 0:
        drawn = block_levels(key, extent, cuts, -0.22, 0.18) * drawn
    return jnp.clip(drawn, min=-reach, max=reach).astype(held_as)


def setup_inputs(seed: int = 0) -> dict:
    arg_keys = jax.random.split(jax.random.key(seed), 16)
    x_in = noise(arg_keys[0], (TOKENS, INNER), 1.0, 6.0, ((0, 256), (1, 4)))
    z_in = noise(arg_keys[1], (TOKENS, INNER), 1.0, 6.0, ((0, 256), (1, 4)))
    b_in = noise(arg_keys[2], (TOKENS, GROUPS * STATE), 0.3, 1.796875, ((0, 256), (1, 4)))
    c_in = noise(arg_keys[3], (TOKENS, GROUPS * STATE), 0.3, 1.796875, ((0, 256), (1, 4)))
    dt_in = draw_dt_in(jax.random.fold_in(arg_keys[15], 71), 0)
    a_log = draw_a_log(jax.random.fold_in(arg_keys[15], 71), 0)
    d_skip = jnp.clip(0.5 + 1.5 * jax.random.uniform(arg_keys[6], (HEADS,), jnp.float32) ** block_levels(arg_keys[6], (HEADS,), ((0, 4),), -0.2, 0.2), 0.5, 2.0)
    norm_w = jnp.clip(1.0 + 0.1 * jax.random.normal(arg_keys[7], (INNER,), jnp.float32), 0.5, 1.5)
    w_out = noise(arg_keys[8], (INNER, D), INNER ** -0.5, 0.09375, ((0, 4),))
    resid = draw_resid(jax.random.fold_in(arg_keys[15], 71), 0)
    routes_keys = jax.random.split(jax.random.fold_in(arg_keys[10], 1), SHARDS * TOK_DEV // ROWS_MOE)
    routes_turns = jax.random.permutation(jax.random.fold_in(arg_keys[10], 3), SHARDS * TOK_DEV // ROWS_MOE)
    routes = jax.vmap(lambda own, number: deal_out(jax.random.fold_in(arg_keys[10], 2), own, number, ROWS_MOE, EXPERTS, TOPK, CAP, 2))(routes_keys, routes_turns).reshape((SHARDS, TOK_DEV, TOPK))
    gates = jnp.clip(0.1 + 0.59999999 * jax.random.uniform(arg_keys[11], (SHARDS, TOK_DEV, TOPK), jnp.float32) ** block_levels(arg_keys[11], (SHARDS, TOK_DEV, TOPK), ((0, 256), (1, 4)), -0.2, 0.2), 0.1, 0.7)
    moe_gain = jnp.clip(1.0 + 0.1 * jax.random.normal(arg_keys[12], (D,), jnp.float32), 0.5, 1.5)
    w_up = noise(arg_keys[13], (EXPERTS, D, FFW), D ** -0.5, 0.15625, ((0, 32),))
    w_down = noise(arg_keys[14], (EXPERTS, FFW, D), FFW ** -0.5, 0.1875, ((0, 32),))
    return dict(x_in=x_in, z_in=z_in, b_in=b_in, c_in=c_in, dt_in=dt_in, a_log=a_log, d_skip=d_skip, norm_w=norm_w, w_out=w_out, resid=resid, routes=routes, gates=gates, moe_gain=moe_gain, w_up=w_up, w_down=w_down)


precise = lax.Precision.HIGHEST

def to_low(values):
    return lax.optimization_barrier(values.astype(jnp.bfloat16)).astype(jnp.float32)

def stretch_pass(carry_state, pieces):
    x_part, b_part, c_part, rate_part, step_part = pieces
    per_group = x_part.shape[1] // b_part.shape[1]
    b_heads = jnp.repeat(b_part, per_group, axis=1).astype(jnp.float32)
    c_heads = jnp.repeat(c_part, per_group, axis=1).astype(jnp.float32)
    x_float = x_part.astype(jnp.float32)
    cumulative = jnp.cumsum(rate_part, axis=0)
    cum_heads = cumulative.T
    distance = cum_heads[:, :, None] - cum_heads[:, None, :]
    length = cumulative.shape[0]
    causal = (jnp.arange(length)[:, None] >= jnp.arange(length)[None, :])[None]
    decay_mat = jnp.where(causal, jnp.exp(jnp.where(causal, distance, 0.0)), 0.0)
    weighting = decay_mat * step_part.T[:, None, :]
    scores = jnp.einsum('thn,shn->hts', c_heads, b_heads, precision=precise)
    mixing = to_low(scores * weighting)
    inside = jnp.einsum('hts,shp->thp', mixing, x_float, precision=precise)
    state_low = to_low(carry_state)
    carried = jnp.exp(cumulative)[:, :, None] * jnp.einsum('thn,hpn->thp', c_heads, state_low, precision=precise)
    tail_weight = jnp.exp(cumulative[-1][None, :] - cumulative) * step_part
    weighted_x = to_low(tail_weight[:, :, None] * x_float)
    update = jnp.einsum('shp,shn->hpn', weighted_x, b_heads, precision=precise)
    new_state = jnp.exp(cumulative[-1])[:, None, None] * carry_state + update
    return (new_state, inside + carried)

def by_stretch(values):
    return values.reshape((values.shape[0] // STRETCH, STRETCH) + values.shape[1:])

def mixer(x_in, z_in, b_in, c_in, dt_in, a_log, d_skip, norm_w):
    length, head_count = dt_in.shape
    groups = b_in.shape[1] // STATE
    low_values = x_in.reshape(length, head_count, HEAD_DIM)
    values = low_values.astype(jnp.float32)
    b_groups = b_in.reshape(length, groups, STATE)
    c_groups = c_in.reshape(length, groups, STATE)
    step_size = jax.nn.softplus(dt_in)
    log_rate = -step_size * jnp.exp(a_log)[None, :]
    zero_state = jnp.zeros((head_count, HEAD_DIM, STATE), jnp.float32)
    last_state, local_out = lax.scan(stretch_pass, zero_state, (by_stretch(low_values), by_stretch(b_groups), by_stretch(c_groups), by_stretch(log_rate), by_stretch(step_size)))
    ssm_out = local_out.reshape(length, head_count, HEAD_DIM) + d_skip[None, :, None] * values
    gated_out = ssm_out * jax.nn.silu(z_in.astype(jnp.float32).reshape(length, head_count, HEAD_DIM))
    grouped = gated_out.reshape(length, groups, -1)
    inverse = lax.rsqrt(lax.optimization_barrier(jnp.mean(grouped * grouped, axis=2, keepdims=True)) + 1e-05)
    return ((grouped * inverse).reshape(length, head_count * HEAD_DIM) * norm_w[None, :]).astype(jnp.bfloat16)

def experts(moe_in, routes, gates, w_up, w_down):
    flat_routes = routes.reshape(-1, TOPK)
    flat_gates = gates.reshape(-1, TOPK)
    length = moe_in.shape[0]
    limit = length // ROWS_MOE * CAP

    def one_expert(summed, expert):
        routed = flat_routes == expert
        weighting = lax.optimization_barrier(jnp.sum(jnp.where(routed, flat_gates, 0.0), axis=1))
        picked = jnp.any(routed, axis=1)
        row_index = jnp.nonzero(picked, size=limit, fill_value=0)[0].astype(jnp.int32)
        row_block = moe_in[row_index].astype(jnp.float32)
        up_proj = jnp.dot(row_block, w_up[expert].astype(jnp.float32), precision=precise, preferred_element_type=jnp.float32)
        activated = jnp.square(jnp.maximum(up_proj, 0.0)).astype(jnp.bfloat16)
        expert_out = jnp.dot(activated.astype(jnp.float32), w_down[expert].astype(jnp.float32), precision=precise, preferred_element_type=jnp.float32).astype(jnp.bfloat16)
        filled = jnp.arange(limit) < jnp.sum(picked.astype(jnp.int32))
        factor = jnp.where(filled, weighting[row_index], 0.0)
        return (summed.at[row_index].add(expert_out.astype(jnp.float32) * factor[:, None]), None)
    start_sum = jnp.zeros((length, moe_in.shape[1]), jnp.float32)
    moe_sum, unused = lax.scan(one_expert, start_sum, jnp.arange(EXPERTS, dtype=jnp.int32))
    return moe_sum

def reference(x_in, z_in, b_in, c_in, dt_in, a_log, d_skip, norm_w, w_out, resid, routes, gates, moe_gain, w_up, w_down):
    normed = mixer(x_in, z_in, b_in, c_in, dt_in, a_log, d_skip, norm_w)
    mixed = jnp.dot(normed, w_out, preferred_element_type=jnp.float32)
    hidden = (resid.reshape(-1, D).astype(jnp.float32) + mixed).astype(jnp.bfloat16)
    hidden_f32 = hidden.astype(jnp.float32)
    inverse = lax.rsqrt(lax.optimization_barrier(jnp.mean(hidden_f32 * hidden_f32, axis=1, keepdims=True)) + 1e-05)
    moe_in = (hidden_f32 * inverse * moe_gain[None, :]).astype(jnp.bfloat16)
    moe_sum = experts(moe_in, routes, gates, w_up, w_down)
    return (hidden_f32 + moe_sum).astype(jnp.bfloat16).reshape(resid.shape)
```

```python
import functools

import jax
import jax.numpy as jnp
from jax import lax
from jax.experimental import pallas as pl
from jax.experimental.pallas import tpu as pltpu
from jax.sharding import PartitionSpec as P

HEAD_DIM = 64
STATE = 128
ROOM = 16
NEAR = 4
F32 = jnp.float32
BF16 = jnp.bfloat16
MESH = pl.DeviceIdType.MESH
EXACT = lax.Precision.HIGHEST


def dot(a, b, ca=1, cb=0, precision=None):
    return lax.dot_general(
        a, b, (((ca,), (cb,)), ((), ())), preferred_element_type=F32, precision=precision
    )


def iota(shape, dim):
    return lax.broadcasted_iota(jnp.int32, shape, dim)


def halves(values):
    high = values.astype(BF16)
    low = (values - high.astype(F32)).astype(BF16)
    return high, low


def kernel(
    sizes,
    x_ref,
    z_ref,
    b_ref,
    c_ref,
    dt_ref,
    alog_ref,
    dskip_ref,
    normw_ref,
    resid_ref,
    routes_ref,
    gates_ref,
    gain_ref,
    wout_hbm,
    wup_hbm,
    wdown_hbm,
    out_ref,
    wout,
    wup,
    wdown,
    wsem,
    y_ref,
    grow_ref,
    pre_ref,
    lpre_ref,
    send_a,
    recv_a,
    sa_sem,
    ra_sem,
    send_n,
    recv_n,
    sn_sem,
    rn_sem,
    pn_ref,
    lpn_ref,
    send_f,
    recv_f,
    sf_sem,
    rf_sem,
    send_m,
    recv_m,
    sm_sem,
    rm_sem,
    send_b,
    recv_b,
    sb_sem,
    rb_sem,
    send_r,
    recv_r,
    sr_sem,
    rr_sem,
    send_d,
    recv_d,
    sd_sem,
    rd_sem,
    send_o,
    recv_o,
    so_sem,
    ro_sem,
):
    n_seq, n_head, n_exp = sizes
    n_far = n_seq // NEAR
    n_plane = n_head * n_exp
    tokens = x_ref.shape[0]
    heads = dt_ref.shape[0]
    groups = b_ref.shape[1] // STATE
    per_group = heads // groups
    width = per_group * HEAD_DIM
    own_heads = heads // n_exp
    own_rows = own_heads * HEAD_DIM
    near_rows = own_rows // NEAR
    rows_here = resid_ref.shape[1]

    me_z = lax.axis_index("seq")
    me_x = lax.axis_index("head")
    me_e = lax.axis_index("exp")
    me_far = me_z // NEAR
    me_near = me_z % NEAR
    me_plane = me_x * n_exp + me_e

    w_copies = [
        pltpu.make_async_copy(wout_hbm, wout, wsem.at[0]),
        pltpu.make_async_copy(wup_hbm, wup, wsem.at[1]),
        pltpu.make_async_copy(wdown_hbm, wdown, wsem.at[2]),
    ]
    for copy in w_copies:
        copy.start()

    def plane_id(d):
        there = lax.rem(me_plane + d, n_plane)
        return there, {"head": there // n_exp, "exp": there % n_exp}

    def exp_id(d):
        there = lax.rem(me_e + d, n_exp)
        return there, {"exp": there}

    def head_id(d):
        there = lax.rem(me_x + d, n_head)
        return there, {"head": there}

    def near_id(d):
        there = lax.rem(me_near + d, NEAR)
        return there, {"seq": me_far * NEAR + there}

    def far_id(d):
        there = lax.rem(me_far + d, n_far)
        return there, {"seq": there * NEAR + me_near}

    barrier = pltpu.get_barrier_semaphore()

    def greet(peer, count):
        def one(d, carry):
            pl.semaphore_signal(barrier, inc=1, device_id=peer(d)[1], device_id_type=MESH)
            return carry

        lax.fori_loop(1, count, one, 0)

    greet(far_id, n_far)
    greet(near_id, NEAR)
    greet(plane_id, n_plane)

    def exchange(peer, count, source, landing, mine, send_sems, recv_sems):
        def copy(there, where):
            return pltpu.make_async_remote_copy(
                src_ref=source.at[there],
                dst_ref=landing.at[mine],
                send_sem=send_sems.at[there],
                recv_sem=recv_sems.at[mine],
                device_id=where,
                device_id_type=MESH,
            )

        def start(d, carry):
            copy(*peer(d)).start()
            return carry

        def sent(d, carry):
            copy(*peer(d)).wait_send()
            return carry

        def arrived(d, carry):
            there, where = peer(d)
            pltpu.make_async_remote_copy(
                src_ref=source.at[there],
                dst_ref=landing.at[there],
                send_sem=send_sems.at[there],
                recv_sem=recv_sems.at[there],
                device_id=where,
                device_id_type=MESH,
            ).wait_recv()
            return carry

        return (
            lambda: lax.fori_loop(1, count, start, 0),
            lambda: lax.fori_loop(1, count, arrived, 0),
            lambda: lax.fori_loop(1, count, sent, 0),
        )

    start_a, arrived_a, sent_a = exchange(exp_id, n_exp, send_a, recv_a, me_e, sa_sem, ra_sem)
    start_n, arrived_n, sent_n = exchange(near_id, NEAR, send_n, recv_n, me_near, sn_sem, rn_sem)
    start_m, arrived_m, sent_m = exchange(near_id, NEAR, send_m, recv_m, me_near, sm_sem, rm_sem)
    start_b, arrived_b, sent_b = exchange(exp_id, n_exp, send_b, recv_b, me_e, sb_sem, rb_sem)
    start_r, arrived_r, sent_r = exchange(head_id, n_head, send_r, recv_r, me_x, sr_sem, rr_sem)
    start_d, arrived_d, sent_d = exchange(
        plane_id, n_plane, send_d, recv_d, me_plane, sd_sem, rd_sem
    )
    start_o, arrived_o, sent_o = exchange(
        plane_id, n_plane, send_o, recv_o, me_plane, so_sem, ro_sem
    )

    dt = dt_ref[...]
    step_t = jnp.maximum(dt, 0.0) + jnp.log1p(jnp.exp(-jnp.abs(dt)))
    decay_rate = jnp.broadcast_to(jnp.exp(alog_ref[...]), (heads, heads))
    same_head = iota((heads, heads), 0) == iota((heads, heads), 1)
    decay_rate = jnp.sum(jnp.where(same_head, decay_rate, 0.0), axis=1, keepdims=True)
    rate_t = -step_t * decay_rate
    row_t, col_t = iota((tokens, tokens), 0), iota((tokens, tokens), 1)
    causal = row_t >= col_t
    upto = jnp.where(causal, 1.0, 0.0)
    cum_t = dot(rate_t, upto, 1, 1, EXACT)
    cum = dot(upto, rate_t, 1, 1, EXACT)
    step = dot(jnp.where(row_t == col_t, 1.0, 0.0), step_t, 1, 1, EXACT)
    tail = jnp.exp(cum[tokens - 1 : tokens, :] - cum) * step
    grow = jnp.exp(cum)
    channels = heads * HEAD_DIM
    spread = jnp.where(
        iota((heads, channels), 1) // HEAD_DIM == iota((heads, channels), 0), 1.0, 0.0
    )
    tail_wide = dot(tail, spread, 1, 0, EXACT)
    weighted = (tail_wide * x_ref[...].astype(F32)).astype(BF16)

    total = jnp.broadcast_to(cum_t[:, tokens - 1 : tokens], (heads, STATE))
    total_high, total_low = halves(total)
    per_send = n_exp // groups
    for g in range(groups):
        update = dot(
            weighted[:, g * width : (g + 1) * width],
            b_ref[:, g * STATE : (g + 1) * STATE],
            0,
            0,
        ).astype(BF16)
        for k in range(per_send):
            send_a[g * per_send + k, 0:own_rows, :] = update[k * own_rows : (k + 1) * own_rows, :]
    for k in range(n_exp):
        send_a[k, own_rows : own_rows + heads, :] = total_high
        send_a[k, own_rows + heads : own_rows + 2 * heads, :] = total_low

    pl.semaphore_wait(barrier, (n_far - 1) + (NEAR - 1) + (n_plane - 1))
    start_a()
    recv_a[me_e] = send_a[me_e]

    first_half = iota((tokens, 2 * HEAD_DIM), 1) < HEAD_DIM
    skip_wide = dot(dskip_ref[...], spread, 1, 0, EXACT)
    for g in range(groups):
        scores = dot(
            c_ref[:, g * STATE : (g + 1) * STATE], b_ref[:, g * STATE : (g + 1) * STATE], 1, 1
        )
        for j in range(g * per_group // 2, (g + 1) * per_group // 2):
            lanes = slice(2 * HEAD_DIM * j, 2 * HEAD_DIM * (j + 1))
            mixes = []
            for h in (2 * j, 2 * j + 1):
                distance = cum[:, h : h + 1] - cum_t[h : h + 1, :]
                decay = jnp.where(causal, jnp.exp(jnp.where(causal, distance, 0.0)), 0.0)
                mixes.append((scores * (decay * step_t[h : h + 1, :])).astype(BF16))
            pair = x_ref[:, lanes]
            zero = jnp.zeros_like(pair)
            stacked = jnp.concatenate(
                [jnp.where(first_half, pair, zero), jnp.where(first_half, zero, pair)], axis=0
            )
            inside = dot(jnp.concatenate(mixes, axis=1), stacked)
            y_ref[:, lanes] = inside + skip_wide[:, lanes] * pair.astype(F32)
    grow_ref[...] = dot(grow, spread, 1, 0, EXACT)

    expert_row = iota((n_plane, rows_here), 0)
    routed = jnp.zeros((n_plane, rows_here), F32)
    gate = jnp.zeros((n_plane, rows_here), F32)
    for k in range(routes_ref.shape[0]):
        hit = expert_row == routes_ref[k : k + 1, :]
        routed = jnp.where(hit, 1.0, routed)
        gate = jnp.where(hit, gates_ref[k : k + 1, :], gate)
    ahead = jnp.where(
        iota((rows_here, rows_here), 0) < iota((rows_here, rows_here), 1), 1.0, 0.0
    ).astype(BF16)
    place = jnp.where(routed > 0.5, dot(routed.astype(BF16), ahead), -1.0)
    slots = n_plane * ROOM
    repeat = jnp.where(
        iota((slots, n_plane), 0) // ROOM == iota((slots, n_plane), 1), 1.0, 0.0
    ).astype(BF16)
    place_wide = dot(repeat, place.astype(BF16))
    chosen = place_wide == (iota((slots, rows_here), 0) % ROOM).astype(F32)
    gate_high, gate_low = halves(gate)
    pick = jnp.where(chosen, 1.0, 0.0).astype(BF16)
    pick_high = jnp.where(chosen, dot(repeat, gate_high), 0.0).astype(BF16)
    pick_low = jnp.where(chosen, dot(repeat, gate_low), 0.0).astype(BF16)

    arrived_a()
    head_row = iota((heads, STATE), 0)
    own_row = iota((own_rows, STATE), 0)
    state = jnp.zeros((own_rows, STATE), F32)
    log_sum = jnp.zeros((own_rows, STATE), F32)
    for k in range(n_exp):
        pre_ref[k] = state
        lpre_ref[k] = log_sum
        high = recv_a[k, own_rows : own_rows + heads, :].astype(F32)
        low = recv_a[k, own_rows + heads : own_rows + 2 * heads, :].astype(F32)
        both = high + low
        log_here = jnp.zeros((own_rows, STATE), F32)
        for h in range(own_heads):
            one = jnp.sum(
                jnp.where(head_row == me_e * own_heads + h, both, 0.0), axis=0, keepdims=True
            )
            log_here = jnp.where(own_row // HEAD_DIM == h, one, log_here)
        state = jnp.exp(log_here) * state + recv_a[k, 0:own_rows, :].astype(F32)
        log_sum = log_sum + log_here

    def packed(values, logs):
        high, low = halves(logs)
        tile = jnp.where(
            iota((16, STATE), 0) < 8,
            jnp.broadcast_to(high.astype(F32), (16, STATE)),
            jnp.broadcast_to(low.astype(F32), (16, STATE)),
        )
        return values.astype(BF16), tile.astype(BF16)

    def unpacked(ref, k):
        tile = ref[k, near_rows : near_rows + 16, :].astype(F32)
        return ref[k, 0:near_rows, :].astype(F32), tile[0:1, :] + tile[8:9, :]

    for k in range(NEAR):
        rows = slice(k * near_rows, (k + 1) * near_rows)
        values, tile = packed(state[rows], log_sum[k * near_rows : k * near_rows + 1])
        send_n[k, 0:near_rows, :] = values
        send_n[k, near_rows : near_rows + 16, :] = tile
    start_n()
    recv_n[me_near] = send_n[me_near]
    arrived_n()
    part = jnp.zeros((near_rows, STATE), F32)
    part_log = jnp.zeros((1, STATE), F32)
    for k in range(NEAR):
        pn_ref[k] = part
        lpn_ref[k] = jnp.broadcast_to(part_log, (8, STATE))
        values, log_here = unpacked(recv_n, k)
        part = jnp.exp(log_here) * part + values
        part_log = part_log + log_here
    values, tile = packed(part, part_log)
    send_f[0:near_rows, :] = values
    send_f[near_rows : near_rows + 16, :] = tile

    def far_copy(there, slot):
        return pltpu.make_async_remote_copy(
            src_ref=send_f,
            dst_ref=recv_f.at[slot],
            send_sem=sf_sem.at[there],
            recv_sem=rf_sem.at[slot],
            device_id={"seq": there * NEAR + me_near},
            device_id_type=MESH,
        )

    def far_start(k, carry):
        far_copy(k, me_far).start()
        return carry

    lax.fori_loop(me_far + 1, n_far, far_start, 0)

    def far_fold(k, carry):
        far_copy(k, k).wait_recv()
        values, log_here = unpacked(recv_f, k)
        return jnp.exp(log_here) * carry + values

    chain = lax.fori_loop(0, me_far, far_fold, jnp.zeros((near_rows, STATE), F32))

    for k in range(NEAR):
        send_m[k] = (jnp.exp(lpn_ref[k, 0:1, :]) * chain + pn_ref[k]).astype(BF16)
    start_m()
    recv_m[me_near] = send_m[me_near]
    arrived_m()
    chain_in = recv_m[...].astype(F32).reshape(own_rows, STATE)
    for k in range(n_exp):
        send_b[k] = (jnp.exp(lpre_ref[k]) * chain_in + pre_ref[k]).astype(BF16)
    start_b()
    recv_b[me_e] = send_b[me_e]
    arrived_b()

    before = recv_b[...].reshape(channels, STATE)
    normed = []
    for g in range(groups):
        lanes = slice(g * width, (g + 1) * width)
        carried = dot(c_ref[:, g * STATE : (g + 1) * STATE], before[lanes], 1, 1)
        ssm_out = y_ref[:, lanes] + grow_ref[:, lanes] * carried
        z_here = z_ref[:, lanes].astype(F32)
        gated = ssm_out * (z_here / (1.0 + jnp.exp(-z_here)))
        inverse = lax.rsqrt(jnp.mean(gated * gated, axis=1, keepdims=True) + 1e-05)
        normed.append((gated * inverse * normw_ref[:, lanes]).astype(BF16))
    normed = jnp.concatenate(normed, axis=1)
    w_copies[0].wait()
    projected = dot(normed, wout[...], 1, 1).astype(BF16)
    for k in range(n_head):
        send_r[k] = projected[k * rows_here : (k + 1) * rows_here]
    start_r()
    recv_r[me_x] = send_r[me_x]
    arrived_r()
    mixed = jnp.sum(recv_r[...].astype(F32), axis=0)
    hidden = (resid_ref[0].astype(F32) + mixed).astype(BF16).astype(F32)
    scale = lax.rsqrt(jnp.mean(hidden * hidden, axis=1, keepdims=True) + 1e-05)
    moe_in = (hidden * scale * gain_ref[...]).astype(BF16)

    model = moe_in.shape[1]
    send_d[...] = dot(pick, moe_in).astype(BF16).reshape(n_plane, ROOM, model)
    start_d()
    recv_d[me_plane] = send_d[me_plane]
    arrived_d()
    w_copies[1].wait()
    w_copies[2].wait()
    rows = recv_d[...].reshape(slots, model)
    raised = jnp.maximum(dot(rows, wup[0], 1, 1), 0.0)
    activated = (raised * raised).astype(BF16)
    send_o[...] = dot(activated, wdown[0]).astype(BF16).reshape(n_plane, ROOM, model)
    start_o()
    recv_o[me_plane] = send_o[me_plane]
    arrived_o()
    returned = recv_o[...].reshape(slots, model)
    moe_sum = dot(pick_high, returned, 0, 0) + dot(pick_low, returned, 0, 0)
    out_ref[0] = (hidden + moe_sum).astype(BF16)

    for sent in (sent_a, sent_n, sent_m, sent_b, sent_r, sent_d, sent_o):
        sent()

    def far_sent(k, carry):
        far_copy(k, me_far).wait_send()
        return carry

    lax.fori_loop(me_far + 1, n_far, far_sent, 0)


def per_device(
    sizes,
    x_in,
    z_in,
    b_in,
    c_in,
    dt_in,
    a_log,
    d_skip,
    norm_w,
    w_out,
    resid,
    routes,
    gates,
    moe_gain,
    w_up,
    w_down,
):
    n_seq, n_head, n_exp = sizes
    n_far, n_plane = n_seq // NEAR, n_head * n_exp
    tokens, heads = dt_in.shape
    channels = heads * HEAD_DIM
    own_rows = channels // n_exp
    near_rows = own_rows // NEAR
    rows_here, model = resid.shape[1:]
    dma = pltpu.SemaphoreType.DMA
    vmem = pl.BlockSpec(memory_space=pltpu.VMEM)
    hbm = pl.BlockSpec(memory_space=pl.ANY)
    w_out_t = w_out.T
    w_up_t = w_up.transpose(0, 2, 1)
    scratch = [
        pltpu.VMEM(w_out_t.shape, BF16),
        pltpu.VMEM(w_up_t.shape, BF16),
        pltpu.VMEM(w_down.shape, BF16),
        dma((3,)),
        pltpu.VMEM((tokens, channels), F32),
        pltpu.VMEM((tokens, channels), F32),
        pltpu.VMEM((n_exp, own_rows, STATE), F32),
        pltpu.VMEM((n_exp, own_rows, STATE), F32),
    ]

    def pair(count, *block):
        return [
            pltpu.VMEM((count, *block), BF16),
            pltpu.VMEM((count, *block), BF16),
            dma((count,)),
            dma((count,)),
        ]

    scratch += pair(n_exp, own_rows + 2 * heads, STATE)
    scratch += pair(NEAR, near_rows + 16, STATE)
    scratch += [
        pltpu.VMEM((NEAR, near_rows, STATE), F32),
        pltpu.VMEM((NEAR, 8, STATE), F32),
        pltpu.VMEM((near_rows + 16, STATE), BF16),
        pltpu.VMEM((n_far, near_rows + 16, STATE), BF16),
        dma((n_far,)),
        dma((n_far,)),
    ]
    scratch += pair(NEAR, near_rows, STATE)
    scratch += pair(n_exp, own_rows, STATE)
    scratch += pair(n_head, rows_here, model)
    scratch += pair(n_plane, ROOM, model)
    scratch += pair(n_plane, ROOM, model)
    return pl.pallas_call(
        functools.partial(kernel, sizes),
        out_shape=jax.ShapeDtypeStruct(resid.shape, BF16),
        in_specs=[vmem] * 12 + [hbm] * 3,
        out_specs=vmem,
        scratch_shapes=scratch,
        compiler_params=pltpu.CompilerParams(
            collective_id=0, has_side_effects=True, vmem_limit_bytes=60 * 2**20
        ),
    )(
        x_in,
        z_in,
        b_in,
        c_in,
        dt_in.T,
        a_log.reshape(1, heads),
        d_skip.reshape(1, heads),
        norm_w.reshape(1, channels),
        resid,
        routes[0].T,
        gates[0].T,
        moe_gain.reshape(1, model),
        w_out_t,
        w_up_t,
        w_down,
    )


def solution(mesh):
    sizes = (mesh.shape["seq"], mesh.shape["head"], mesh.shape["exp"])
    placed = (
        P(("seq", "exp"), "head"),
        P(("seq", "exp"), "head"),
        P(("seq", "exp"), "head"),
        P(("seq", "exp"), "head"),
        P(("seq", "exp"), "head"),
        P("head"),
        P("head"),
        P("head"),
        P("head", None),
        P(("seq", "exp"), "head", None),
        P(("seq", "exp"), "head", None),
        P(("seq", "exp"), "head", None),
        P(),
        P(("head", "exp"), None, None),
        P(("head", "exp"), None, None),
    )
    return jax.shard_map(
        functools.partial(per_device, sizes),
        mesh=mesh,
        in_specs=placed,
        out_specs=P(("seq", "exp"), "head", None),
        check_vma=False,
    )
```

```python
import functools

import jax
import jax.numpy as jnp
from jax import lax
from jax.experimental import pallas as pl
from jax.experimental.pallas import tpu as pltpu
from jax.sharding import PartitionSpec as P

HEAD_DIM = 64
STATE = 128
ROOM = 16
NEAR = 4
F32 = jnp.float32
BF16 = jnp.bfloat16
REACH = (1, 2, -1, -2)
MESH = pl.DeviceIdType.MESH
EXACT = lax.Precision.HIGHEST


def dot(a, b, ca=1, cb=0, precision=None):
    return lax.dot_general(
        a, b, (((ca,), (cb,)), ((), ())), preferred_element_type=F32, precision=precision
    )


def iota(shape, dim):
    return lax.broadcasted_iota(jnp.int32, shape, dim)


def halves(values):
    high = values.astype(BF16)
    low = (values - high.astype(F32)).astype(BF16)
    return high, low


def kernel(
    sizes,
    x_ref,
    z_ref,
    b_ref,
    c_ref,
    dt_ref,
    alog_ref,
    dskip_ref,
    normw_ref,
    resid_ref,
    routes_ref,
    gates_ref,
    gain_ref,
    wout_hbm,
    wup_hbm,
    wdown_hbm,
    out_ref,
    wout,
    wup,
    wdown,
    wsem,
    y_ref,
    grow_ref,
    pre_ref,
    lpre_ref,
    send_a,
    recv_a,
    sa_sem,
    ra_sem,
    send_n,
    recv_n,
    sn_sem,
    rn_sem,
    pn_ref,
    lpn_ref,
    send_f,
    recv_f,
    sf_sem,
    rf_sem,
    send_m,
    recv_m,
    sm_sem,
    rm_sem,
    send_b,
    recv_b,
    sb_sem,
    rb_sem,
    send_r,
    recv_r,
    sr_sem,
    rr_sem,
    send_d,
    recv_d,
    sd_sem,
    rd_sem,
    send_o,
    recv_o,
    so_sem,
    ro_sem,
):
    n_seq, n_head, n_exp = sizes
    n_far = n_seq // NEAR
    assert n_far in (1, 8)
    n_plane = n_head * n_exp
    tokens = x_ref.shape[0]
    heads = dt_ref.shape[0]
    groups = b_ref.shape[1] // STATE
    per_group = heads // groups
    width = per_group * HEAD_DIM
    own_heads = heads // n_exp
    own_rows = own_heads * HEAD_DIM
    near_rows = own_rows // NEAR
    rows_here = resid_ref.shape[1]

    me_z = lax.axis_index("seq")
    me_x = lax.axis_index("head")
    me_e = lax.axis_index("exp")
    me_far = me_z // NEAR
    me_near = me_z % NEAR
    me_plane = me_x * n_exp + me_e

    w_copies = [
        pltpu.make_async_copy(wout_hbm, wout, wsem.at[0]),
        pltpu.make_async_copy(wup_hbm, wup, wsem.at[1]),
        pltpu.make_async_copy(wdown_hbm, wdown, wsem.at[2]),
    ]
    for copy in w_copies:
        copy.start()

    def plane_id(d):
        there = lax.rem(me_plane + d, n_plane)
        return there, {"head": there // n_exp, "exp": there % n_exp}

    def exp_id(d):
        there = lax.rem(me_e + d, n_exp)
        return there, {"exp": there}

    def head_id(d):
        there = lax.rem(me_x + d, n_head)
        return there, {"head": there}

    def near_id(d):
        there = lax.rem(me_near + d, NEAR)
        return there, {"seq": me_far * NEAR + there}

    def far_id(d):
        there = lax.rem(me_far + d + n_far, n_far)
        return {"seq": there * NEAR + me_near}

    barrier = pltpu.get_barrier_semaphore()

    def greet(peer, count):
        def one(d, carry):
            pl.semaphore_signal(barrier, inc=1, device_id=peer(d)[1], device_id_type=MESH)
            return carry

        lax.fori_loop(1, count, one, 0)

    if n_far > 1:
        for d in REACH:
            pl.semaphore_signal(barrier, inc=1, device_id=far_id(d), device_id_type=MESH)
    greet(near_id, NEAR)
    greet(plane_id, n_plane)

    def exchange(peer, count, source, landing, mine, send_sems, recv_sems):
        def copy(there, where):
            return pltpu.make_async_remote_copy(
                src_ref=source.at[there],
                dst_ref=landing.at[mine],
                send_sem=send_sems.at[there],
                recv_sem=recv_sems.at[mine],
                device_id=where,
                device_id_type=MESH,
            )

        def start(d, carry):
            copy(*peer(d)).start()
            return carry

        def sent(d, carry):
            copy(*peer(d)).wait_send()
            return carry

        def arrived(d, carry):
            there, where = peer(d)
            pltpu.make_async_remote_copy(
                src_ref=source.at[there],
                dst_ref=landing.at[there],
                send_sem=send_sems.at[there],
                recv_sem=recv_sems.at[there],
                device_id=where,
                device_id_type=MESH,
            ).wait_recv()
            return carry

        return (
            lambda: lax.fori_loop(1, count, start, 0),
            lambda: lax.fori_loop(1, count, arrived, 0),
            lambda: lax.fori_loop(1, count, sent, 0),
        )

    start_a, arrived_a, sent_a = exchange(exp_id, n_exp, send_a, recv_a, me_e, sa_sem, ra_sem)
    start_n, arrived_n, sent_n = exchange(near_id, NEAR, send_n, recv_n, me_near, sn_sem, rn_sem)
    start_m, arrived_m, sent_m = exchange(near_id, NEAR, send_m, recv_m, me_near, sm_sem, rm_sem)
    start_b, arrived_b, sent_b = exchange(exp_id, n_exp, send_b, recv_b, me_e, sb_sem, rb_sem)
    start_r, arrived_r, sent_r = exchange(head_id, n_head, send_r, recv_r, me_x, sr_sem, rr_sem)
    start_d, arrived_d, sent_d = exchange(
        plane_id, n_plane, send_d, recv_d, me_plane, sd_sem, rd_sem
    )
    start_o, arrived_o, sent_o = exchange(
        plane_id, n_plane, send_o, recv_o, me_plane, so_sem, ro_sem
    )

    dt = dt_ref[...]
    step_t = jnp.maximum(dt, 0.0) + jnp.log1p(jnp.exp(-jnp.abs(dt)))
    decay_rate = jnp.broadcast_to(jnp.exp(alog_ref[...]), (heads, heads))
    same_head = iota((heads, heads), 0) == iota((heads, heads), 1)
    decay_rate = jnp.sum(jnp.where(same_head, decay_rate, 0.0), axis=1, keepdims=True)
    rate_t = -step_t * decay_rate
    row_t, col_t = iota((tokens, tokens), 0), iota((tokens, tokens), 1)
    causal = row_t >= col_t
    upto = jnp.where(causal, 1.0, 0.0)
    cum_t = dot(rate_t, upto, 1, 1, EXACT)
    cum = dot(upto, rate_t, 1, 1, EXACT)
    step = dot(jnp.where(row_t == col_t, 1.0, 0.0), step_t, 1, 1, EXACT)
    tail = jnp.exp(cum[tokens - 1 : tokens, :] - cum) * step
    grow = jnp.exp(cum)
    channels = heads * HEAD_DIM
    spread = jnp.where(
        iota((heads, channels), 1) // HEAD_DIM == iota((heads, channels), 0), 1.0, 0.0
    )
    tail_wide = dot(tail, spread, 1, 0, EXACT)
    weighted = (tail_wide * x_ref[...].astype(F32)).astype(BF16)

    total = jnp.broadcast_to(cum_t[:, tokens - 1 : tokens], (heads, STATE))
    total_high, total_low = halves(total)
    per_send = n_exp // groups
    for g in range(groups):
        update = dot(
            weighted[:, g * width : (g + 1) * width],
            b_ref[:, g * STATE : (g + 1) * STATE],
            0,
            0,
        ).astype(BF16)
        for k in range(per_send):
            send_a[g * per_send + k, 0:own_rows, :] = update[k * own_rows : (k + 1) * own_rows, :]
    for k in range(n_exp):
        send_a[k, own_rows : own_rows + heads, :] = total_high
        send_a[k, own_rows + heads : own_rows + 2 * heads, :] = total_low

    pl.semaphore_wait(barrier, (len(REACH) if n_far > 1 else 0) + (NEAR - 1) + (n_plane - 1))
    start_a()
    recv_a[me_e] = send_a[me_e]

    first_half = iota((tokens, 2 * HEAD_DIM), 1) < HEAD_DIM
    skip_wide = dot(dskip_ref[...], spread, 1, 0, EXACT)
    for g in range(groups):
        scores = dot(
            c_ref[:, g * STATE : (g + 1) * STATE], b_ref[:, g * STATE : (g + 1) * STATE], 1, 1
        )
        for j in range(g * per_group // 2, (g + 1) * per_group // 2):
            lanes = slice(2 * HEAD_DIM * j, 2 * HEAD_DIM * (j + 1))
            mixes = []
            for h in (2 * j, 2 * j + 1):
                distance = cum[:, h : h + 1] - cum_t[h : h + 1, :]
                decay = jnp.where(causal, jnp.exp(jnp.where(causal, distance, 0.0)), 0.0)
                mixes.append((scores * (decay * step_t[h : h + 1, :])).astype(BF16))
            pair = x_ref[:, lanes]
            zero = jnp.zeros_like(pair)
            stacked = jnp.concatenate(
                [jnp.where(first_half, pair, zero), jnp.where(first_half, zero, pair)], axis=0
            )
            inside = dot(jnp.concatenate(mixes, axis=1), stacked)
            y_ref[:, lanes] = inside + skip_wide[:, lanes] * pair.astype(F32)
    grow_ref[...] = dot(grow, spread, 1, 0, EXACT)

    expert_row = iota((n_plane, rows_here), 0)
    routed = jnp.zeros((n_plane, rows_here), F32)
    gate = jnp.zeros((n_plane, rows_here), F32)
    for k in range(routes_ref.shape[0]):
        hit = expert_row == routes_ref[k]
        routed = jnp.where(hit, 1.0, routed)
        gate = jnp.where(hit, gates_ref[k], gate)
    ahead = jnp.where(
        iota((rows_here, rows_here), 0) < iota((rows_here, rows_here), 1), 1.0, 0.0
    ).astype(BF16)
    place = jnp.where(routed > 0.5, dot(routed.astype(BF16), ahead), -1.0)
    slots = n_plane * ROOM
    repeat = jnp.where(
        iota((slots, n_plane), 0) // ROOM == iota((slots, n_plane), 1), 1.0, 0.0
    ).astype(BF16)
    place_wide = dot(repeat, place.astype(BF16))
    chosen = place_wide == (iota((slots, rows_here), 0) % ROOM).astype(F32)
    gate_high, gate_low = halves(gate)
    pick = jnp.where(chosen, 1.0, 0.0).astype(BF16)
    pick_high = jnp.where(chosen, dot(repeat, gate_high), 0.0).astype(BF16)
    pick_low = jnp.where(chosen, dot(repeat, gate_low), 0.0).astype(BF16)

    arrived_a()
    head_row = iota((heads, STATE), 0)
    own_row = iota((own_rows, STATE), 0)
    state = jnp.zeros((own_rows, STATE), F32)
    log_sum = jnp.zeros((own_rows, STATE), F32)
    for k in range(n_exp):
        pre_ref[k] = state
        lpre_ref[k] = log_sum
        high = recv_a[k, own_rows : own_rows + heads, :].astype(F32)
        low = recv_a[k, own_rows + heads : own_rows + 2 * heads, :].astype(F32)
        both = high + low
        log_here = jnp.zeros((own_rows, STATE), F32)
        for h in range(own_heads):
            one = jnp.sum(
                jnp.where(head_row == me_e * own_heads + h, both, 0.0), axis=0, keepdims=True
            )
            log_here = jnp.where(own_row // HEAD_DIM == h, one, log_here)
        state = jnp.exp(log_here) * state + recv_a[k, 0:own_rows, :].astype(F32)
        log_sum = log_sum + log_here

    def packed(values, logs):
        high, low = halves(logs)
        tile = jnp.where(
            iota((16, STATE), 0) < 8,
            jnp.broadcast_to(high.astype(F32), (16, STATE)),
            jnp.broadcast_to(low.astype(F32), (16, STATE)),
        )
        return values.astype(BF16), tile.astype(BF16)

    def unpacked(ref, k):
        tile = ref[k, near_rows : near_rows + 16, :].astype(F32)
        return ref[k, 0:near_rows, :].astype(F32), tile[0:1, :] + tile[8:9, :]

    for k in range(NEAR):
        rows = slice(k * near_rows, (k + 1) * near_rows)
        values, tile = packed(state[rows], log_sum[k * near_rows : k * near_rows + 1])
        send_n[k, 0:near_rows, :] = values
        send_n[k, near_rows : near_rows + 16, :] = tile
    start_n()
    recv_n[me_near] = send_n[me_near]
    arrived_n()
    part = jnp.zeros((near_rows, STATE), F32)
    part_log = jnp.zeros((1, STATE), F32)
    for k in range(NEAR):
        pn_ref[k] = part
        lpn_ref[k] = jnp.broadcast_to(part_log, (8, STATE))
        values, log_here = unpacked(recv_n, k)
        part = jnp.exp(log_here) * part + values
        part_log = part_log + log_here
    chain = jnp.zeros((near_rows, STATE), F32)

    def put(slot, values, logs):
        values, tile = packed(values, logs)
        send_f[slot, 0:near_rows, :] = values
        send_f[slot, near_rows : near_rows + 16, :] = tile

    def far_copy(d, source, slot):
        return pltpu.make_async_remote_copy(
            src_ref=send_f.at[source],
            dst_ref=recv_f.at[slot],
            send_sem=sf_sem.at[slot],
            recv_sem=rf_sem.at[slot],
            device_id=far_id(d),
            device_id_type=MESH,
        )

    if n_far > 1:
        put(0, part, part_log)
        copies = [far_copy(d, 0, slot) for slot, d in enumerate(REACH)]
        for copy in copies:
            copy.start()
        for copy in copies[:3]:
            copy.wait_recv()
        one, one_log = unpacked(recv_f, 0)
        two, two_log = unpacked(recv_f, 1)
        two = jnp.where(me_far >= 2, two, 0.0)
        two_log = jnp.where(me_far >= 2, two_log, 0.0)
        fold = jnp.where(me_far >= 1, jnp.exp(one_log) * two + one, 0.0)
        fold_log = jnp.where(me_far >= 1, one_log + two_log, 0.0)
        put(1, fold, fold_log)
        copies.append(far_copy(2, 1, 4))
        copies[4].start()
        back, back_log = unpacked(recv_f, 2)
        put(2, back, back_log)
        copies.append(far_copy(-2, 2, 5))
        copies[5].start()
        for copy in copies[3:]:
            copy.wait_recv()
        for slot, least in ((2, 7), (3, 6), (5, 5), (4, 2), (1, 2), (0, 1)):
            values, log_here = unpacked(recv_f, slot)
            chain = jnp.where(me_far >= least, jnp.exp(log_here) * chain + values, chain)

    for k in range(NEAR):
        send_m[k] = (jnp.exp(lpn_ref[k, 0:1, :]) * chain + pn_ref[k]).astype(BF16)
    start_m()
    recv_m[me_near] = send_m[me_near]
    arrived_m()
    chain_in = recv_m[...].astype(F32).reshape(own_rows, STATE)
    for k in range(n_exp):
        send_b[k] = (jnp.exp(lpre_ref[k]) * chain_in + pre_ref[k]).astype(BF16)
    start_b()
    recv_b[me_e] = send_b[me_e]
    arrived_b()

    before = recv_b[...].reshape(channels, STATE)
    normed = []
    for g in range(groups):
        lanes = slice(g * width, (g + 1) * width)
        carried = dot(c_ref[:, g * STATE : (g + 1) * STATE], before[lanes], 1, 1)
        ssm_out = y_ref[:, lanes] + grow_ref[:, lanes] * carried
        z_here = z_ref[:, lanes].astype(F32)
        gated = ssm_out * (z_here / (1.0 + jnp.exp(-z_here)))
        inverse = lax.rsqrt(jnp.mean(gated * gated, axis=1, keepdims=True) + 1e-05)
        normed.append((gated * inverse * normw_ref[:, lanes]).astype(BF16))
    normed = jnp.concatenate(normed, axis=1)
    w_copies[0].wait()
    projected = dot(normed, wout[...], 1, 1).astype(BF16)
    for k in range(n_head):
        send_r[k] = projected[k * rows_here : (k + 1) * rows_here]
    start_r()
    recv_r[me_x] = send_r[me_x]
    arrived_r()
    mixed = jnp.sum(recv_r[...].astype(F32), axis=0)
    hidden = (resid_ref[0].astype(F32) + mixed).astype(BF16).astype(F32)
    scale = lax.rsqrt(jnp.mean(hidden * hidden, axis=1, keepdims=True) + 1e-05)
    moe_in = (hidden * scale * gain_ref[...].reshape(1, -1)).astype(BF16)

    model = moe_in.shape[1]
    send_d[...] = dot(pick, moe_in).astype(BF16).reshape(n_plane, ROOM, model)
    start_d()
    recv_d[me_plane] = send_d[me_plane]
    arrived_d()
    w_copies[1].wait()
    w_copies[2].wait()
    rows = recv_d[...].reshape(slots, model)
    raised = jnp.maximum(dot(rows, wup[0], 1, 1), 0.0)
    activated = (raised * raised).astype(BF16)
    send_o[...] = dot(activated, wdown[0]).astype(BF16).reshape(n_plane, ROOM, model)
    start_o()
    recv_o[me_plane] = send_o[me_plane]
    arrived_o()
    returned = recv_o[...].reshape(slots, model)
    moe_sum = dot(pick_high, returned, 0, 0) + dot(pick_low, returned, 0, 0)
    out_ref[0] = (hidden + moe_sum).astype(BF16)

    for sent in (sent_a, sent_n, sent_m, sent_b, sent_r, sent_d, sent_o):
        sent()

    if n_far > 1:
        for copy in copies:
            copy.wait_send()


def per_device(
    sizes,
    x_in,
    z_in,
    b_in,
    c_in,
    dt_in,
    a_log,
    d_skip,
    norm_w,
    w_out,
    resid,
    routes,
    gates,
    moe_gain,
    w_up,
    w_down,
):
    n_seq, n_head, n_exp = sizes
    n_plane = n_head * n_exp
    tokens, heads = dt_in.shape
    channels = heads * HEAD_DIM
    own_rows = channels // n_exp
    near_rows = own_rows // NEAR
    rows_here, model = resid.shape[1:]
    dma = pltpu.SemaphoreType.DMA
    vmem = pl.BlockSpec(memory_space=pltpu.VMEM)
    hbm = pl.BlockSpec(memory_space=pl.ANY)
    w_out_t = w_out.T
    w_up_t = w_up.transpose(0, 2, 1)
    scratch = [
        pltpu.VMEM(w_out_t.shape, BF16),
        pltpu.VMEM(w_up_t.shape, BF16),
        pltpu.VMEM(w_down.shape, BF16),
        dma((3,)),
        pltpu.VMEM((tokens, channels), F32),
        pltpu.VMEM((tokens, channels), F32),
        pltpu.VMEM((n_exp, own_rows, STATE), F32),
        pltpu.VMEM((n_exp, own_rows, STATE), F32),
    ]

    def pair(count, *block):
        return [
            pltpu.VMEM((count, *block), BF16),
            pltpu.VMEM((count, *block), BF16),
            dma((count,)),
            dma((count,)),
        ]

    scratch += pair(n_exp, own_rows + 2 * heads, STATE)
    scratch += pair(NEAR, near_rows + 16, STATE)
    scratch += [
        pltpu.VMEM((NEAR, near_rows, STATE), F32),
        pltpu.VMEM((NEAR, 8, STATE), F32),
        pltpu.VMEM((3, near_rows + 16, STATE), BF16),
        pltpu.VMEM((6, near_rows + 16, STATE), BF16),
        dma((6,)),
        dma((6,)),
    ]
    scratch += pair(NEAR, near_rows, STATE)
    scratch += pair(n_exp, own_rows, STATE)
    scratch += pair(n_head, rows_here, model)
    scratch += pair(n_plane, ROOM, model)
    scratch += pair(n_plane, ROOM, model)
    return pl.pallas_call(
        functools.partial(kernel, sizes),
        out_shape=jax.ShapeDtypeStruct(resid.shape, BF16),
        in_specs=[vmem] * 12 + [hbm] * 3,
        out_specs=vmem,
        scratch_shapes=scratch,
        compiler_params=pltpu.CompilerParams(
            collective_id=0, has_side_effects=True, vmem_limit_bytes=60 * 2**20
        ),
    )(
        x_in,
        z_in,
        b_in,
        c_in,
        dt_in.T,
        a_log.reshape(1, heads),
        d_skip.reshape(1, heads),
        norm_w.reshape(1, channels),
        resid,
        routes.transpose(2, 0, 1),
        gates.transpose(2, 0, 1),
        moe_gain,
        w_out_t,
        w_up_t,
        w_down,
    )


def solution(mesh):
    sizes = (mesh.shape["seq"], mesh.shape["head"], mesh.shape["exp"])
    placed = (
        P(("seq", "exp"), "head"),
        P(("seq", "exp"), "head"),
        P(("seq", "exp"), "head"),
        P(("seq", "exp"), "head"),
        P(("seq", "exp"), "head"),
        P("head"),
        P("head"),
        P("head"),
        P("head", None),
        P(("seq", "exp"), "head", None),
        P(("seq", "exp"), "head", None),
        P(("seq", "exp"), "head", None),
        P(),
        P(("head", "exp"), None, None),
        P(("head", "exp"), None, None),
    )
    return jax.shard_map(
        functools.partial(per_device, sizes),
        mesh=mesh,
        in_specs=placed,
        out_specs=P(("seq", "exp"), "head", None),
        check_vma=False,
    )
```

```python
import functools

import jax
import jax.numpy as jnp
from jax import lax
from jax.experimental import pallas as pl
from jax.experimental.pallas import tpu as pltpu
from jax.sharding import PartitionSpec as P

HEAD_DIM = 64
STATE = 128
ROOM = 16
CORES = 2
NEAR = 4
F32 = jnp.float32
BF16 = jnp.bfloat16
REACH = (1, 2, -1, -2)
MESH = pl.DeviceIdType.MESH
EXACT = lax.Precision.HIGHEST


def dot(a, b, ca=1, cb=0, precision=None):
    return lax.dot_general(
        a, b, (((ca,), (cb,)), ((), ())), preferred_element_type=F32, precision=precision
    )


def iota(shape, dim):
    return lax.broadcasted_iota(jnp.int32, shape, dim)


def halves(values):
    high = values.astype(BF16)
    low = (values - high.astype(F32)).astype(BF16)
    return high, low


def kernel(
    sizes,
    x_ref,
    z_ref,
    b_ref,
    c_ref,
    dt_ref,
    alog_ref,
    dskip_ref,
    normw_ref,
    resid_ref,
    routes_ref,
    gates_ref,
    gain_ref,
    wout_hbm,
    wup_hbm,
    wdown_hbm,
    out_ref,
    wout,
    wup,
    wdown,
    wsem,
    y_ref,
    grow_ref,
    pre_ref,
    lpre_ref,
    send_a,
    recv_a,
    sa_sem,
    ra_sem,
    send_n,
    recv_n,
    sn_sem,
    rn_sem,
    pn_ref,
    lpn_ref,
    send_f,
    recv_f,
    sf_sem,
    rf_sem,
    send_m,
    recv_m,
    sm_sem,
    rm_sem,
    send_b,
    recv_b,
    sb_sem,
    rb_sem,
    send_r,
    recv_r,
    sr_sem,
    rr_sem,
    table_x,
    tables_x,
    tx_send,
    tx_recv,
    table_y,
    tables_y,
    ty_send,
    ty_recv,
    pick_x,
    pick_y,
    half_x,
    gathered_x,
    gx_send,
    gx_recv,
    half_y,
    gathered_y,
    gy_send,
    gy_recv,
    rows_x,
    landed_x,
    lx_send,
    lx_recv,
    rows_y,
    landed_y,
    ly_send,
    ly_recv,
    made_x,
    back_x,
    bx_send,
    bx_recv,
    made_y,
    back_y,
    by_send,
    by_recv,
    sums_x,
    last_x,
    fx_send,
    fx_recv,
    sums_y,
    last_y,
    fy_send,
    fy_recv,
):
    n_seq, n_head, n_exp = sizes
    n_far = n_seq // NEAR
    assert n_far in (1, 8)
    n_plane = n_head * n_exp
    tokens = x_ref.shape[0]
    heads = dt_ref.shape[0]
    groups = b_ref.shape[1] // STATE
    per_group = heads // groups
    width = per_group * HEAD_DIM
    own_heads = heads // n_exp
    own_rows = own_heads * HEAD_DIM
    near_rows = own_rows // NEAR
    rows_here = resid_ref.shape[1]

    me_z = lax.axis_index("seq")
    me_x = lax.axis_index("head")
    me_e = lax.axis_index("exp")
    me_far = me_z // NEAR
    me_near = me_z % NEAR
    n_y = n_exp // CORES
    me_y = me_e // CORES
    me_c = me_e % CORES
    me_block = me_x * CORES + me_c

    w_copies = [
        pltpu.make_async_copy(wout_hbm, wout, wsem.at[0]),
        pltpu.make_async_copy(wup_hbm, wup, wsem.at[1]),
        pltpu.make_async_copy(wdown_hbm, wdown, wsem.at[2]),
    ]
    for copy in w_copies:
        copy.start()

    def exp_id(d):
        there = lax.rem(me_e + d, n_exp)
        return there, {"exp": there}

    def head_id(d):
        there = lax.rem(me_x + d, n_head)
        return there, {"head": there}

    def y_id(d):
        there = lax.rem(me_y + d, n_y)
        return there, {"exp": there * CORES + me_c}

    def block_id(d):
        there = lax.rem(me_block + d, n_head * CORES)
        return there, {"head": there // CORES, "exp": me_y * CORES + there % CORES}

    def near_id(d):
        there = lax.rem(me_near + d, NEAR)
        return there, {"seq": me_far * NEAR + there}

    def far_id(d):
        there = lax.rem(me_far + d + n_far, n_far)
        return {"seq": there * NEAR + me_near}

    barrier = pltpu.get_barrier_semaphore()

    def greet(peer, count):
        def one(d, carry):
            pl.semaphore_signal(barrier, inc=1, device_id=peer(d)[1], device_id_type=MESH)
            return carry

        lax.fori_loop(1, count, one, 0)

    if n_far > 1:
        for d in REACH:
            pl.semaphore_signal(barrier, inc=1, device_id=far_id(d), device_id_type=MESH)
    greet(near_id, NEAR)
    greet(exp_id, n_exp)
    for d in range(1, n_head):
        for core in range(CORES):
            where = {"head": lax.rem(me_x + d, n_head), "exp": me_y * CORES + core}
            pl.semaphore_signal(barrier, inc=1, device_id=where, device_id_type=MESH)

    def exchange(peer, count, source, landing, mine, send_sems, recv_sems):
        def copy(there, where, place):
            return pltpu.make_async_remote_copy(
                src_ref=source(there),
                dst_ref=landing(place),
                send_sem=send_sems.at[there],
                recv_sem=recv_sems.at[place],
                device_id=where,
                device_id_type=MESH,
            )

        def start(d, carry):
            there, where = peer(d)
            copy(there, where, mine).start()
            return carry

        def sent(d, carry):
            there, where = peer(d)
            copy(there, where, mine).wait_send()
            return carry

        def arrived(d, carry):
            there, where = peer(d)
            copy(there, where, there).wait_recv()
            return carry

        return (
            lambda: lax.fori_loop(1, count, start, 0),
            lambda: lax.fori_loop(1, count, arrived, 0),
            lambda: lax.fori_loop(1, count, sent, 0),
        )

    def at(ref):
        return lambda k: ref.at[k]

    def whole(ref):
        return lambda k: ref

    def across(ref):
        return lambda k: ref.at[:, k % CORES, k // CORES]

    start_a, arrived_a, sent_a = exchange(
        exp_id, n_exp, at(send_a), at(recv_a), me_e, sa_sem, ra_sem
    )
    start_n, arrived_n, sent_n = exchange(
        near_id, NEAR, at(send_n), at(recv_n), me_near, sn_sem, rn_sem
    )
    start_m, arrived_m, sent_m = exchange(
        near_id, NEAR, at(send_m), at(recv_m), me_near, sm_sem, rm_sem
    )
    start_b, arrived_b, sent_b = exchange(
        exp_id, n_exp, at(send_b), at(recv_b), me_e, sb_sem, rb_sem
    )
    start_r, arrived_r, sent_r = exchange(
        head_id, n_head, at(send_r), at(recv_r), me_x, sr_sem, rr_sem
    )
    start_tx, arrived_tx, sent_tx = exchange(
        head_id, n_head, whole(table_x), at(tables_x), me_x, tx_send, tx_recv
    )
    start_ty, arrived_ty, sent_ty = exchange(
        y_id, n_y, whole(table_y), at(tables_y), me_y, ty_send, ty_recv
    )
    start_gx, arrived_gx, sent_gx = exchange(
        head_id, n_head, whole(half_x), at(gathered_x), me_x, gx_send, gx_recv
    )
    start_gy, arrived_gy, sent_gy = exchange(
        y_id, n_y, whole(half_y), at(gathered_y), me_y, gy_send, gy_recv
    )
    start_lx, arrived_lx, sent_lx = exchange(
        exp_id, n_exp, at(rows_x), at(landed_x), me_e, lx_send, lx_recv
    )
    start_ly, arrived_ly, sent_ly = exchange(
        block_id, n_head * CORES, at(rows_y), across(landed_y), me_block, ly_send, ly_recv
    )
    start_bx, arrived_bx, sent_bx = exchange(
        exp_id, n_exp, at(made_x), at(back_x), me_e, bx_send, bx_recv
    )
    start_by, arrived_by, sent_by = exchange(
        block_id, n_head * CORES, across(made_y), at(back_y), me_block, by_send, by_recv
    )
    start_fx, arrived_fx, sent_fx = exchange(
        head_id, n_head, at(sums_x), at(last_x), me_x, fx_send, fx_recv
    )
    start_fy, arrived_fy, sent_fy = exchange(
        y_id, n_y, at(sums_y), at(last_y), me_y, fy_send, fy_recv
    )

    dt = dt_ref[...]
    step_t = jnp.maximum(dt, 0.0) + jnp.log1p(jnp.exp(-jnp.abs(dt)))
    decay_rate = jnp.broadcast_to(jnp.exp(alog_ref[...]), (heads, heads))
    same_head = iota((heads, heads), 0) == iota((heads, heads), 1)
    decay_rate = jnp.sum(jnp.where(same_head, decay_rate, 0.0), axis=1, keepdims=True)
    rate_t = -step_t * decay_rate
    row_t, col_t = iota((tokens, tokens), 0), iota((tokens, tokens), 1)
    causal = row_t >= col_t
    upto = jnp.where(causal, 1.0, 0.0)
    cum_t = dot(rate_t, upto, 1, 1, EXACT)
    cum = dot(upto, rate_t, 1, 1, EXACT)
    step = dot(jnp.where(row_t == col_t, 1.0, 0.0), step_t, 1, 1, EXACT)
    tail = jnp.exp(cum[tokens - 1 : tokens, :] - cum) * step
    grow = jnp.exp(cum)
    channels = heads * HEAD_DIM
    spread = jnp.where(
        iota((heads, channels), 1) // HEAD_DIM == iota((heads, channels), 0), 1.0, 0.0
    )
    tail_wide = dot(tail, spread, 1, 0, EXACT)
    weighted = (tail_wide * x_ref[...].astype(F32)).astype(BF16)

    total = jnp.broadcast_to(cum_t[:, tokens - 1 : tokens], (heads, STATE))
    total_high, total_low = halves(total)
    per_send = n_exp // groups
    for g in range(groups):
        update = dot(
            weighted[:, g * width : (g + 1) * width],
            b_ref[:, g * STATE : (g + 1) * STATE],
            0,
            0,
        ).astype(BF16)
        for k in range(per_send):
            send_a[g * per_send + k, 0:own_rows, :] = update[k * own_rows : (k + 1) * own_rows, :]
    tile_row = iota((n_exp * 16, 2 * heads), 0)
    its_head = tile_row // 16 * own_heads + tile_row % own_heads + heads * (tile_row % 16 // 8)
    logs = dot(
        jnp.where(its_head == iota((n_exp * 16, 2 * heads), 1), 1.0, 0.0).astype(BF16),
        jnp.concatenate([total_high, total_low], axis=0),
    ).astype(BF16)
    for k in range(n_exp):
        send_a[k, own_rows : own_rows + 16, :] = logs[k * 16 : (k + 1) * 16]

    expert_row = iota((n_plane, rows_here), 0)
    routed = jnp.zeros((n_plane, rows_here), F32)
    gate = jnp.zeros((n_plane, rows_here), F32)
    for k in range(routes_ref.shape[0]):
        hit = expert_row == routes_ref[k]
        routed = jnp.where(hit, 1.0, routed)
        gate = jnp.where(hit, gates_ref[k], gate)
    upto_here = jnp.where(
        iota((rows_here, rows_here), 0) <= iota((rows_here, rows_here), 1), 1.0, 0.0
    ).astype(BF16)
    place = routed * dot(routed.astype(BF16), upto_here)
    gate_high, gate_low = halves(gate)
    table = jnp.concatenate([place.astype(BF16), gate_high, gate_low], axis=0)

    def in_lanes(count, mine):
        lanes = (rows_here, count * rows_here)
        spot = iota(lanes, 1) == iota(lanes, 0) + mine * rows_here
        return dot(table, jnp.where(spot, 1.0, 0.0).astype(BF16)).astype(BF16)

    table_x[...] = in_lanes(n_head, me_x)
    table_y[...] = in_lanes(n_y, me_y)

    far_peers = len(REACH) if n_far > 1 else 0
    pl.semaphore_wait(barrier, far_peers + (NEAR - 1) + (n_exp - 1) + (n_head - 1) * CORES)
    start_a()
    recv_a[me_e] = send_a[me_e]
    start_tx()
    start_ty()
    tables_x[me_x] = table_x[...]
    tables_y[me_y] = table_y[...]

    first_half = iota((tokens, 2 * HEAD_DIM), 1) < HEAD_DIM
    skip_wide = dot(dskip_ref[...], spread, 1, 0, EXACT)
    for g in range(groups):
        scores = dot(
            c_ref[:, g * STATE : (g + 1) * STATE], b_ref[:, g * STATE : (g + 1) * STATE], 1, 1
        )
        for j in range(g * per_group // 2, (g + 1) * per_group // 2):
            lanes = slice(2 * HEAD_DIM * j, 2 * HEAD_DIM * (j + 1))
            mixes = []
            for h in (2 * j, 2 * j + 1):
                distance = cum[:, h : h + 1] - cum_t[h : h + 1, :]
                decay = jnp.where(causal, jnp.exp(jnp.where(causal, distance, 0.0)), 0.0)
                mixes.append((scores * (decay * step_t[h : h + 1, :])).astype(BF16))
            pair = x_ref[:, lanes]
            zero = jnp.zeros_like(pair)
            stacked = jnp.concatenate(
                [jnp.where(first_half, pair, zero), jnp.where(first_half, zero, pair)], axis=0
            )
            inside = dot(jnp.concatenate(mixes, axis=1), stacked)
            y_ref[:, lanes] = inside + skip_wide[:, lanes] * pair.astype(F32)
    grow_ref[...] = dot(grow, spread, 1, 0, EXACT)

    arrived_a()
    own_row = iota((own_rows, STATE), 0)
    state = jnp.zeros((own_rows, STATE), F32)
    log_sum = jnp.zeros((own_rows, STATE), F32)
    for k in range(n_exp):
        pre_ref[k] = state
        lpre_ref[k] = log_sum
        tile = recv_a[k, own_rows : own_rows + 16, :].astype(F32)
        log_here = jnp.zeros((own_rows, STATE), F32)
        for h in range(own_heads):
            one = tile[h : h + 1, :] + tile[8 + h : 9 + h, :]
            log_here = jnp.where(own_row // HEAD_DIM == h, one, log_here)
        state = jnp.exp(log_here) * state + recv_a[k, 0:own_rows, :].astype(F32)
        log_sum = log_sum + log_here

    def packed(values, logs):
        high, low = halves(logs)
        tile = jnp.where(
            iota((16, STATE), 0) < 8,
            jnp.broadcast_to(high.astype(F32), (16, STATE)),
            jnp.broadcast_to(low.astype(F32), (16, STATE)),
        )
        return values.astype(BF16), tile.astype(BF16)

    def unpacked(ref, k):
        tile = ref[k, near_rows : near_rows + 16, :].astype(F32)
        return ref[k, 0:near_rows, :].astype(F32), tile[0:1, :] + tile[8:9, :]

    for k in range(NEAR):
        rows = slice(k * near_rows, (k + 1) * near_rows)
        values, tile = packed(state[rows], log_sum[k * near_rows : k * near_rows + 1])
        send_n[k, 0:near_rows, :] = values
        send_n[k, near_rows : near_rows + 16, :] = tile
    start_n()
    recv_n[me_near] = send_n[me_near]
    arrived_n()
    part = jnp.zeros((near_rows, STATE), F32)
    part_log = jnp.zeros((1, STATE), F32)
    for k in range(NEAR):
        pn_ref[k] = part
        lpn_ref[k] = jnp.broadcast_to(part_log, (8, STATE))
        values, log_here = unpacked(recv_n, k)
        part = jnp.exp(log_here) * part + values
        part_log = part_log + log_here
    chain = jnp.zeros((near_rows, STATE), F32)

    def put(slot, values, logs):
        values, tile = packed(values, logs)
        send_f[slot, 0:near_rows, :] = values
        send_f[slot, near_rows : near_rows + 16, :] = tile

    def far_copy(d, source, slot):
        return pltpu.make_async_remote_copy(
            src_ref=send_f.at[source],
            dst_ref=recv_f.at[slot],
            send_sem=sf_sem.at[slot],
            recv_sem=rf_sem.at[slot],
            device_id=far_id(d),
            device_id_type=MESH,
        )

    def choose(tables, pick, expert, inner):
        row, lane = iota(pick.shape[1:], 0), iota(pick.shape[1:], 1)
        slots = pick.shape[1]
        wanted = expert(iota((slots, n_plane), 0) // (inner * ROOM))
        repeat = jnp.where(wanted == iota((slots, n_plane), 1), 1.0, 0.0).astype(BF16)
        every = jnp.sum(tables[...].astype(F32), axis=0).astype(BF16)
        spot = dot(repeat, every[0:n_plane])
        chosen = (spot == (row % ROOM + 1).astype(F32)) & (
            row // ROOM % inner == lane // rows_here
        )
        pick[0] = jnp.where(chosen, 1.0, 0.0).astype(BF16)
        for part in (1, 2):
            wide = dot(repeat, every[part * n_plane : (part + 1) * n_plane])
            pick[part] = jnp.where(chosen, wide, 0.0).astype(BF16)

    def choose_both():
        arrived_tx()
        arrived_ty()
        choose(tables_x, pick_x, lambda k: me_x * n_exp + k, n_head)
        choose(
            tables_y,
            pick_y,
            lambda k: k // CORES * n_exp + me_y * CORES + k % CORES,
            n_y,
        )

    if n_far == 1:
        choose_both()
    if n_far > 1:
        put(0, part, part_log)
        copies = [far_copy(d, 0, slot) for slot, d in enumerate(REACH)]
        copies += [far_copy(2, 1, 4), far_copy(-2, 2, 5)]
        early = me_far <= 1
        relays = early | (me_far == 7)
        goes = (
            me_far <= 6,
            me_far <= 5,
            me_far <= 2,
            early,
            (me_far >= 1) & (me_far <= 5),
            relays,
        )
        comes = (me_far >= 1, me_far >= 2, relays, me_far >= 6, me_far >= 3, me_far >= 5)

        def only(slots, flags, act):
            for slot in slots:
                pl.when(flags[slot])(functools.partial(act, copies[slot]))

        only((1, 0, 3, 2), goes, lambda copy: copy.start())
        choose_both()
        only((0, 1, 2), comes, lambda copy: copy.wait_recv())
        one, one_log = unpacked(recv_f, 0)
        two, two_log = unpacked(recv_f, 1)
        two = jnp.where(me_far >= 2, two, 0.0)
        two_log = jnp.where(me_far >= 2, two_log, 0.0)
        fold = jnp.where(me_far >= 1, jnp.exp(one_log) * two + one, 0.0)
        fold_log = jnp.where(me_far >= 1, one_log + two_log, 0.0)
        put(1, fold, fold_log)
        only((4,), goes, lambda copy: copy.start())
        back, back_log = unpacked(recv_f, 2)
        put(2, back, back_log)
        only((5,), goes, lambda copy: copy.start())
        only((3, 4, 5), comes, lambda copy: copy.wait_recv())
        for slot, least in ((2, 7), (3, 6), (5, 5), (4, 3), (1, 2), (0, 1)):
            values, log_here = unpacked(recv_f, slot)
            chain = jnp.where(me_far >= least, jnp.exp(log_here) * chain + values, chain)

    for k in range(NEAR):
        send_m[k] = (jnp.exp(lpn_ref[k, 0:1, :]) * chain + pn_ref[k]).astype(BF16)
    start_m()
    recv_m[me_near] = send_m[me_near]
    arrived_m()
    chain_in = recv_m[...].astype(F32).reshape(own_rows, STATE)
    for k in range(n_exp):
        send_b[k] = (jnp.exp(lpre_ref[k]) * chain_in + pre_ref[k]).astype(BF16)
    start_b()
    recv_b[me_e] = send_b[me_e]
    arrived_b()

    before = recv_b[...].reshape(channels, STATE)
    normed = []
    for g in range(groups):
        lanes = slice(g * width, (g + 1) * width)
        carried = dot(c_ref[:, g * STATE : (g + 1) * STATE], before[lanes], 1, 1)
        ssm_out = y_ref[:, lanes] + grow_ref[:, lanes] * carried
        z_here = z_ref[:, lanes].astype(F32)
        gated = ssm_out * (z_here / (1.0 + jnp.exp(-z_here)))
        inverse = lax.rsqrt(jnp.mean(gated * gated, axis=1, keepdims=True) + 1e-05)
        normed.append((gated * inverse * normw_ref[:, lanes]).astype(BF16))
    normed = jnp.concatenate(normed, axis=1)
    w_copies[0].wait()
    projected = dot(normed, wout[...], 1, 1).astype(BF16)
    for k in range(n_head):
        send_r[k] = projected[k * rows_here : (k + 1) * rows_here]
    start_r()
    recv_r[me_x] = send_r[me_x]
    arrived_r()
    mixed = jnp.sum(recv_r[...].astype(F32), axis=0)
    hidden = (resid_ref[0].astype(F32) + mixed).astype(BF16).astype(F32)
    scale = lax.rsqrt(jnp.mean(hidden * hidden, axis=1, keepdims=True) + 1e-05)
    moe_in = (hidden * scale * gain_ref[...].reshape(1, -1)).astype(BF16)

    model = moe_in.shape[1]
    split = half_x.shape[1]
    half_x[...] = moe_in[:, :split]
    half_y[...] = moe_in[:, split:]
    start_gx()
    start_gy()
    gathered_x[me_x] = half_x[...]
    gathered_y[me_y] = half_y[...]
    arrived_gx()
    picked = dot(pick_x[0], gathered_x[...].reshape(n_head * rows_here, split))
    rows_x[...] = picked.astype(BF16).reshape(rows_x.shape)
    start_lx()
    arrived_gy()
    picked = dot(pick_y[0], gathered_y[...].reshape(n_y * rows_here, model - split))
    rows_y[...] = picked.astype(BF16).reshape(rows_y.shape)
    start_ly()
    landed_x[me_e] = rows_x[me_e]
    landed_y[:, me_c, me_x] = rows_y[me_block]
    w_copies[1].wait()
    w_copies[2].wait()
    slots = n_plane * ROOM
    arrived_lx()
    raised = dot(landed_x[...].reshape(slots, split), wup[0, :, :split], 1, 1)
    arrived_ly()
    raised += dot(landed_y[...].reshape(slots, model - split), wup[0, :, split:], 1, 1)
    raised = jnp.maximum(raised, 0.0)
    activated = (raised * raised).astype(BF16)

    made_x[...] = dot(activated, wdown[0, :, :split]).astype(BF16).reshape(made_x.shape)
    start_bx()
    made_y[...] = dot(activated, wdown[0, :, split:]).astype(BF16).reshape(made_y.shape)
    start_by()
    back_x[me_e] = made_x[me_e]
    back_y[me_block] = made_y[:, me_c, me_x]
    arrived_bx()
    back = back_x[...].reshape(slots, split)
    summed = dot(pick_x[1], back, 0, 0) + dot(pick_x[2], back, 0, 0)
    sums_x[...] = summed.astype(BF16).reshape(sums_x.shape)
    start_fx()
    arrived_by()
    back = back_y[...].reshape(slots, model - split)
    summed = dot(pick_y[1], back, 0, 0) + dot(pick_y[2], back, 0, 0)
    sums_y[...] = summed.astype(BF16).reshape(sums_y.shape)
    start_fy()
    last_x[me_x] = sums_x[me_x]
    last_y[me_y] = sums_y[me_y]
    arrived_fx()
    moe_sum = jnp.sum(last_x[...].astype(F32), axis=0)
    out_ref[0, :, :split] = (hidden[:, :split] + moe_sum).astype(BF16)
    arrived_fy()
    moe_sum = jnp.sum(last_y[...].astype(F32), axis=0)
    out_ref[0, :, split:] = (hidden[:, split:] + moe_sum).astype(BF16)

    for sent in (sent_a, sent_tx, sent_ty, sent_n, sent_m, sent_b, sent_r):
        sent()
    for sent in (sent_gx, sent_gy, sent_lx, sent_ly, sent_bx, sent_by, sent_fx, sent_fy):
        sent()

    if n_far > 1:
        only(range(6), goes, lambda copy: copy.wait_send())


def per_device(
    sizes,
    x_in,
    z_in,
    b_in,
    c_in,
    dt_in,
    a_log,
    d_skip,
    norm_w,
    w_out,
    resid,
    routes,
    gates,
    moe_gain,
    w_up,
    w_down,
):
    n_seq, n_head, n_exp = sizes
    n_plane = n_head * n_exp
    tokens, heads = dt_in.shape
    channels = heads * HEAD_DIM
    own_rows = channels // n_exp
    near_rows = own_rows // NEAR
    rows_here, model = resid.shape[1:]
    dma = pltpu.SemaphoreType.DMA
    vmem = pl.BlockSpec(memory_space=pltpu.VMEM)
    hbm = pl.BlockSpec(memory_space=pl.ANY)
    w_out_t = w_out.T
    w_up_t = w_up.transpose(0, 2, 1)
    scratch = [
        pltpu.VMEM(w_out_t.shape, BF16),
        pltpu.VMEM(w_up_t.shape, BF16),
        pltpu.VMEM(w_down.shape, BF16),
        dma((3,)),
        pltpu.VMEM((tokens, channels), F32),
        pltpu.VMEM((tokens, channels), F32),
        pltpu.VMEM((n_exp, own_rows, STATE), F32),
        pltpu.VMEM((n_exp, own_rows, STATE), F32),
    ]

    def pair(count, *block):
        return [
            pltpu.VMEM((count, *block), BF16),
            pltpu.VMEM((count, *block), BF16),
            dma((count,)),
            dma((count,)),
        ]

    scratch += pair(n_exp, own_rows + 16, STATE)
    scratch += pair(NEAR, near_rows + 16, STATE)
    scratch += [
        pltpu.VMEM((NEAR, near_rows, STATE), F32),
        pltpu.VMEM((NEAR, 8, STATE), F32),
        pltpu.VMEM((3, near_rows + 16, STATE), BF16),
        pltpu.VMEM((6, near_rows + 16, STATE), BF16),
        dma((6,)),
        dma((6,)),
    ]
    scratch += pair(NEAR, near_rows, STATE)
    scratch += pair(n_exp, own_rows, STATE)
    scratch += pair(n_head, rows_here, model)
    n_y = n_exp // CORES
    split = model // 256 * 128
    rest = model - split
    slots = n_plane * ROOM

    def crossing(source, landing, count):
        return [pltpu.VMEM(source, BF16), pltpu.VMEM(landing, BF16), dma((count,)), dma((count,))]

    table = (3 * n_plane, n_head * rows_here)
    scratch += crossing(table, (n_head, *table), n_head)
    table = (3 * n_plane, n_y * rows_here)
    scratch += crossing(table, (n_y, *table), n_y)
    scratch += [
        pltpu.VMEM((3, slots, n_head * rows_here), BF16),
        pltpu.VMEM((3, slots, n_y * rows_here), BF16),
    ]
    scratch += crossing((rows_here, split), (n_head, rows_here, split), n_head)
    scratch += crossing((rows_here, rest), (n_y, rows_here, rest), n_y)
    by_exp = (n_exp, n_head, ROOM, split)
    by_block = (n_head * CORES, n_y, ROOM, rest)
    by_source = (n_y, CORES, n_head, ROOM, rest)
    scratch += crossing(by_exp, by_exp, n_exp)
    scratch += crossing(by_block, by_source, n_head * CORES)
    scratch += crossing(by_exp, by_exp, n_exp)
    scratch += crossing(by_source, by_block, n_head * CORES)
    scratch += pair(n_head, rows_here, split)
    scratch += pair(n_y, rows_here, rest)
    return pl.pallas_call(
        functools.partial(kernel, sizes),
        out_shape=jax.ShapeDtypeStruct(resid.shape, BF16),
        in_specs=[vmem] * 12 + [hbm] * 3,
        out_specs=vmem,
        scratch_shapes=scratch,
        compiler_params=pltpu.CompilerParams(
            collective_id=0, has_side_effects=True, vmem_limit_bytes=60 * 2**20
        ),
    )(
        x_in,
        z_in,
        b_in,
        c_in,
        dt_in.T,
        a_log.reshape(1, heads),
        d_skip.reshape(1, heads),
        norm_w.reshape(1, channels),
        resid,
        routes.transpose(2, 0, 1),
        gates.transpose(2, 0, 1),
        moe_gain,
        w_out_t,
        w_up_t,
        w_down,
    )


def solution(mesh):
    sizes = (mesh.shape["seq"], mesh.shape["head"], mesh.shape["exp"])
    placed = (
        P(("seq", "exp"), "head"),
        P(("seq", "exp"), "head"),
        P(("seq", "exp"), "head"),
        P(("seq", "exp"), "head"),
        P(("seq", "exp"), "head"),
        P("head"),
        P("head"),
        P("head"),
        P("head", None),
        P(("seq", "exp"), "head", None),
        P(("seq", "exp"), "head", None),
        P(("seq", "exp"), "head", None),
        P(),
        P(("head", "exp"), None, None),
        P(("head", "exp"), None, None),
    )
    return jax.shard_map(
        functools.partial(per_device, sizes),
        mesh=mesh,
        in_specs=placed,
        out_specs=P(("seq", "exp"), "head", None),
        check_vma=False,
    )
```

```python
import functools

import jax
import jax.numpy as jnp
from jax import lax
from jax.experimental import pallas as pl
from jax.experimental.pallas import tpu as pltpu
from jax.sharding import PartitionSpec as P

HEAD_DIM = 64
STATE = 128
ROOM = 16
CORES = 2
NEAR = 4
OWN = {1: (0, 2, 4, 5, 6), 2: (4, 5), 3: (3, 4), 4: (3,), 5: (2,)}
UPTO = {1: (1, 3), 2: (1, 3), 6: (1,)}
RELAY = (7, 2)
LANDS = ((1,), (2, 3, 7), (3, 6, 7), (4, 5, 6, 7), (5, 6, 7), (6, 7), (7,))
F32 = jnp.float32
BF16 = jnp.bfloat16
MESH = pl.DeviceIdType.MESH
EXACT = lax.Precision.HIGHEST


def dot(a, b, ca=1, cb=0, precision=None):
    return lax.dot_general(
        a, b, (((ca,), (cb,)), ((), ())), preferred_element_type=F32, precision=precision
    )


def iota(shape, dim):
    return lax.broadcasted_iota(jnp.int32, shape, dim)


def halves(values):
    high = values.astype(BF16)
    low = (values - high.astype(F32)).astype(BF16)
    return high, low


def kernel(
    sizes,
    x_ref,
    z_ref,
    b_ref,
    c_ref,
    dt_ref,
    alog_ref,
    dskip_ref,
    normw_ref,
    resid_ref,
    routes_ref,
    gates_ref,
    gain_ref,
    wout_hbm,
    wup_hbm,
    wdown_hbm,
    out_ref,
    wout,
    wup,
    wdown,
    wsem,
    y_ref,
    grow_ref,
    pre_ref,
    lpre_ref,
    send_a,
    recv_a,
    sa_sem,
    ra_sem,
    send_n,
    recv_n,
    sn_sem,
    rn_sem,
    pn_ref,
    lpn_ref,
    send_f,
    recv_f,
    sf_sem,
    rf_sem,
    send_m,
    recv_m,
    sm_sem,
    rm_sem,
    send_b,
    recv_b,
    sb_sem,
    rb_sem,
    send_r,
    recv_r,
    sr_sem,
    rr_sem,
    table_x,
    tables_x,
    tx_send,
    tx_recv,
    table_y,
    tables_y,
    ty_send,
    ty_recv,
    pick_x,
    pick_y,
    half_x,
    gathered_x,
    gx_send,
    gx_recv,
    half_y,
    gathered_y,
    gy_send,
    gy_recv,
    rows_x,
    landed_x,
    lx_send,
    lx_recv,
    rows_y,
    landed_y,
    ly_send,
    ly_recv,
    made_x,
    back_x,
    bx_send,
    bx_recv,
    made_y,
    back_y,
    by_send,
    by_recv,
    sums_x,
    last_x,
    fx_send,
    fx_recv,
    sums_y,
    last_y,
    fy_send,
    fy_recv,
):
    n_seq, n_head, n_exp = sizes
    n_far = n_seq // NEAR
    n_plane = n_head * n_exp
    tokens = x_ref.shape[0]
    heads = dt_ref.shape[0]
    groups = b_ref.shape[1] // STATE
    per_group = heads // groups
    width = per_group * HEAD_DIM
    own_heads = heads // n_exp
    own_rows = own_heads * HEAD_DIM
    near_rows = own_rows // NEAR
    rows_here = resid_ref.shape[1]

    me_z = lax.axis_index("seq")
    me_x = lax.axis_index("head")
    me_e = lax.axis_index("exp")
    me_far = me_z // NEAR
    me_near = me_z % NEAR
    n_y = n_exp // CORES
    me_y = me_e // CORES
    me_c = me_e % CORES
    me_block = me_x * CORES + me_c

    w_copies = [
        pltpu.make_async_copy(wout_hbm, wout, wsem.at[0]),
        pltpu.make_async_copy(wup_hbm, wup, wsem.at[1]),
        pltpu.make_async_copy(wdown_hbm, wdown, wsem.at[2]),
    ]
    for copy in w_copies:
        copy.start()

    def exp_id(d):
        there = lax.rem(me_e + d, n_exp)
        return there, {"exp": there}

    def head_id(d):
        there = lax.rem(me_x + d, n_head)
        return there, {"head": there}

    def y_id(d):
        there = lax.rem(me_y + d, n_y)
        return there, {"exp": there * CORES + me_c}

    def block_id(d):
        there = lax.rem(me_block + d, n_head * CORES)
        return there, {"head": there // CORES, "exp": me_y * CORES + there % CORES}

    def near_id(d):
        there = lax.rem(me_near + d, NEAR)
        return there, {"seq": me_far * NEAR + there}

    def far_id(d):
        return {"seq": (me_far + d) * NEAR + me_near}

    barrier = pltpu.get_barrier_semaphore()

    def greet(peer, count):
        def one(d, carry):
            pl.semaphore_signal(barrier, inc=1, device_id=peer(d)[1], device_id_type=MESH)
            return carry

        lax.fori_loop(1, count, one, 0)

    def member(set_of):
        found = me_far < 0
        for group in set_of:
            found = found | (me_far == group)
        return found

    def greet_far(d):
        pl.semaphore_signal(barrier, inc=1, device_id=far_id(d), device_id_type=MESH)

    far_peers = 0
    if n_far > 1:
        assert n_far == len(LANDS) + 1
        for d in range(1, n_far):
            low = set(OWN.get(d, ())) | set(UPTO.get(d, ()))
            for there, ends in ((d, low), (-d, {group + d for group in low})):
                if ends:
                    meets = member(sorted(ends))
                    pl.when(meets)(functools.partial(greet_far, there))
                    far_peers = far_peers + jnp.where(meets, 1, 0)
    greet(near_id, NEAR)
    greet(exp_id, n_exp)
    for d in range(1, n_head):
        for core in range(CORES):
            where = {"head": lax.rem(me_x + d, n_head), "exp": me_y * CORES + core}
            pl.semaphore_signal(barrier, inc=1, device_id=where, device_id_type=MESH)

    def exchange(peer, count, source, landing, mine, send_sems, recv_sems):
        def copy(there, where, place):
            return pltpu.make_async_remote_copy(
                src_ref=source(there),
                dst_ref=landing(place),
                send_sem=send_sems.at[there],
                recv_sem=recv_sems.at[place],
                device_id=where,
                device_id_type=MESH,
            )

        def start(d, carry):
            there, where = peer(d)
            copy(there, where, mine).start()
            return carry

        def sent(d, carry):
            there, where = peer(d)
            copy(there, where, mine).wait_send()
            return carry

        def arrived(d, carry):
            there, where = peer(d)
            copy(there, where, there).wait_recv()
            return carry

        return (
            lambda: lax.fori_loop(1, count, start, 0),
            lambda: lax.fori_loop(1, count, arrived, 0),
            lambda: lax.fori_loop(1, count, sent, 0),
        )

    def at(ref):
        return lambda k: ref.at[k]

    def whole(ref):
        return lambda k: ref

    def across(ref):
        return lambda k: ref.at[:, k % CORES, k // CORES]

    start_a, arrived_a, sent_a = exchange(
        exp_id, n_exp, at(send_a), at(recv_a), me_e, sa_sem, ra_sem
    )
    start_n, arrived_n, sent_n = exchange(
        near_id, NEAR, at(send_n), at(recv_n), me_near, sn_sem, rn_sem
    )
    start_m, arrived_m, sent_m = exchange(
        near_id, NEAR, at(send_m), at(recv_m), me_near, sm_sem, rm_sem
    )
    start_b, arrived_b, sent_b = exchange(
        exp_id, n_exp, at(send_b), at(recv_b), me_e, sb_sem, rb_sem
    )
    start_r, arrived_r, sent_r = exchange(
        head_id, n_head, at(send_r), at(recv_r), me_x, sr_sem, rr_sem
    )
    start_tx, arrived_tx, sent_tx = exchange(
        head_id, n_head, whole(table_x), at(tables_x), me_x, tx_send, tx_recv
    )
    start_ty, arrived_ty, sent_ty = exchange(
        y_id, n_y, whole(table_y), at(tables_y), me_y, ty_send, ty_recv
    )
    start_gx, arrived_gx, sent_gx = exchange(
        head_id, n_head, whole(half_x), at(gathered_x), me_x, gx_send, gx_recv
    )
    start_gy, arrived_gy, sent_gy = exchange(
        y_id, n_y, whole(half_y), at(gathered_y), me_y, gy_send, gy_recv
    )
    start_lx, arrived_lx, sent_lx = exchange(
        exp_id, n_exp, at(rows_x), at(landed_x), me_e, lx_send, lx_recv
    )
    start_ly, arrived_ly, sent_ly = exchange(
        block_id, n_head * CORES, at(rows_y), across(landed_y), me_block, ly_send, ly_recv
    )
    start_bx, arrived_bx, sent_bx = exchange(
        exp_id, n_exp, at(made_x), at(back_x), me_e, bx_send, bx_recv
    )
    start_by, arrived_by, sent_by = exchange(
        block_id, n_head * CORES, across(made_y), at(back_y), me_block, by_send, by_recv
    )
    start_fx, arrived_fx, sent_fx = exchange(
        head_id, n_head, at(sums_x), at(last_x), me_x, fx_send, fx_recv
    )
    start_fy, arrived_fy, sent_fy = exchange(
        y_id, n_y, at(sums_y), at(last_y), me_y, fy_send, fy_recv
    )

    dt = dt_ref[...]
    step_t = jnp.maximum(dt, 0.0) + jnp.log1p(jnp.exp(-jnp.abs(dt)))
    decay_rate = jnp.broadcast_to(jnp.exp(alog_ref[...]), (heads, heads))
    same_head = iota((heads, heads), 0) == iota((heads, heads), 1)
    decay_rate = jnp.sum(jnp.where(same_head, decay_rate, 0.0), axis=1, keepdims=True)
    rate_t = -step_t * decay_rate
    row_t, col_t = iota((tokens, tokens), 0), iota((tokens, tokens), 1)
    causal = row_t >= col_t
    upto = jnp.where(causal, 1.0, 0.0)
    cum_t = dot(rate_t, upto, 1, 1, EXACT)
    cum = dot(upto, rate_t, 1, 1, EXACT)
    step = dot(jnp.where(row_t == col_t, 1.0, 0.0), step_t, 1, 1, EXACT)
    tail = jnp.exp(cum[tokens - 1 : tokens, :] - cum) * step
    grow = jnp.exp(cum)
    channels = heads * HEAD_DIM
    spread = jnp.where(
        iota((heads, channels), 1) // HEAD_DIM == iota((heads, channels), 0), 1.0, 0.0
    )
    tail_wide = dot(tail, spread, 1, 0, EXACT)
    weighted = (tail_wide * x_ref[...].astype(F32)).astype(BF16)

    total = jnp.broadcast_to(cum_t[:, tokens - 1 : tokens], (heads, STATE))
    total_high, total_low = halves(total)
    per_send = n_exp // groups
    for g in range(groups):
        update = dot(
            weighted[:, g * width : (g + 1) * width],
            b_ref[:, g * STATE : (g + 1) * STATE],
            0,
            0,
        ).astype(BF16)
        for k in range(per_send):
            send_a[g * per_send + k, 0:own_rows, :] = update[k * own_rows : (k + 1) * own_rows, :]
    tile_row = iota((n_exp * 16, 2 * heads), 0)
    its_head = tile_row // 16 * own_heads + tile_row % own_heads + heads * (tile_row % 16 // 8)
    logs = dot(
        jnp.where(its_head == iota((n_exp * 16, 2 * heads), 1), 1.0, 0.0).astype(BF16),
        jnp.concatenate([total_high, total_low], axis=0),
    ).astype(BF16)
    for k in range(n_exp):
        send_a[k, own_rows : own_rows + 16, :] = logs[k * 16 : (k + 1) * 16]

    expert_row = iota((n_plane, rows_here), 0)
    routed = jnp.zeros((n_plane, rows_here), F32)
    gate = jnp.zeros((n_plane, rows_here), F32)
    for k in range(routes_ref.shape[0]):
        hit = expert_row == routes_ref[k]
        routed = jnp.where(hit, 1.0, routed)
        gate = jnp.where(hit, gates_ref[k], gate)
    upto_here = jnp.where(
        iota((rows_here, rows_here), 0) <= iota((rows_here, rows_here), 1), 1.0, 0.0
    ).astype(BF16)
    place = routed * dot(routed.astype(BF16), upto_here)
    gate_high, gate_low = halves(gate)
    table = jnp.concatenate([place.astype(BF16), gate_high, gate_low], axis=0)

    def in_lanes(count, mine):
        lanes = (rows_here, count * rows_here)
        spot = iota(lanes, 1) == iota(lanes, 0) + mine * rows_here
        return dot(table, jnp.where(spot, 1.0, 0.0).astype(BF16)).astype(BF16)

    table_x[...] = in_lanes(n_head, me_x)
    table_y[...] = in_lanes(n_y, me_y)

    pl.semaphore_wait(barrier, far_peers + (NEAR - 1) + (n_exp - 1) + (n_head - 1) * CORES)
    start_a()
    recv_a[me_e] = send_a[me_e]
    start_tx()
    start_ty()
    tables_x[me_x] = table_x[...]
    tables_y[me_y] = table_y[...]

    first_half = iota((tokens, 2 * HEAD_DIM), 1) < HEAD_DIM
    skip_wide = dot(dskip_ref[...], spread, 1, 0, EXACT)
    for g in range(groups):
        scores = dot(
            c_ref[:, g * STATE : (g + 1) * STATE], b_ref[:, g * STATE : (g + 1) * STATE], 1, 1
        )
        for j in range(g * per_group // 2, (g + 1) * per_group // 2):
            lanes = slice(2 * HEAD_DIM * j, 2 * HEAD_DIM * (j + 1))
            mixes = []
            for h in (2 * j, 2 * j + 1):
                distance = cum[:, h : h + 1] - cum_t[h : h + 1, :]
                decay = jnp.where(causal, jnp.exp(jnp.where(causal, distance, 0.0)), 0.0)
                mixes.append((scores * (decay * step_t[h : h + 1, :])).astype(BF16))
            pair = x_ref[:, lanes]
            zero = jnp.zeros_like(pair)
            stacked = jnp.concatenate(
                [jnp.where(first_half, pair, zero), jnp.where(first_half, zero, pair)], axis=0
            )
            inside = dot(jnp.concatenate(mixes, axis=1), stacked)
            y_ref[:, lanes] = inside + skip_wide[:, lanes] * pair.astype(F32)
    grow_ref[...] = dot(grow, spread, 1, 0, EXACT)

    arrived_a()
    own_row = iota((own_rows, STATE), 0)
    state = jnp.zeros((own_rows, STATE), F32)
    log_sum = jnp.zeros((own_rows, STATE), F32)
    for k in range(n_exp):
        pre_ref[k] = state
        lpre_ref[k] = log_sum
        tile = recv_a[k, own_rows : own_rows + 16, :].astype(F32)
        log_here = jnp.zeros((own_rows, STATE), F32)
        for h in range(own_heads):
            one = tile[h : h + 1, :] + tile[8 + h : 9 + h, :]
            log_here = jnp.where(own_row // HEAD_DIM == h, one, log_here)
        state = jnp.exp(log_here) * state + recv_a[k, 0:own_rows, :].astype(F32)
        log_sum = log_sum + log_here

    def packed(values, logs):
        high, low = halves(logs)
        tile = jnp.where(
            iota((16, STATE), 0) < 8,
            jnp.broadcast_to(high.astype(F32), (16, STATE)),
            jnp.broadcast_to(low.astype(F32), (16, STATE)),
        )
        return values.astype(BF16), tile.astype(BF16)

    def unpacked(ref, k):
        tile = ref[k, near_rows : near_rows + 16, :].astype(F32)
        return ref[k, 0:near_rows, :].astype(F32), tile[0:1, :] + tile[8:9, :]

    for k in range(NEAR):
        rows = slice(k * near_rows, (k + 1) * near_rows)
        values, tile = packed(state[rows], log_sum[k * near_rows : k * near_rows + 1])
        send_n[k, 0:near_rows, :] = values
        send_n[k, near_rows : near_rows + 16, :] = tile
    start_n()
    recv_n[me_near] = send_n[me_near]
    arrived_n()
    part = jnp.zeros((near_rows, STATE), F32)
    part_log = jnp.zeros((1, STATE), F32)
    for k in range(NEAR):
        pn_ref[k] = part
        lpn_ref[k] = jnp.broadcast_to(part_log, (8, STATE))
        values, log_here = unpacked(recv_n, k)
        part = jnp.exp(log_here) * part + values
        part_log = part_log + log_here
    def far_copy(d, source, slot, sem):
        return pltpu.make_async_remote_copy(
            src_ref=send_f.at[source],
            dst_ref=recv_f.at[slot],
            send_sem=sf_sem.at[sem],
            recv_sem=rf_sem.at[slot],
            device_id=far_id(d),
            device_id_type=MESH,
        )

    def put(slot, values, tile):
        send_f[slot, 0:near_rows, :] = values.astype(BF16)
        send_f[slot, near_rows : near_rows + 16, :] = tile

    final = jnp.full((16, STATE), -16384.0, BF16)
    far_sends = []

    def choose(tables, pick, expert, inner):
        row, lane = iota(pick.shape[1:], 0), iota(pick.shape[1:], 1)
        slots = pick.shape[1]
        wanted = expert(iota((slots, n_plane), 0) // (inner * ROOM))
        repeat = jnp.where(wanted == iota((slots, n_plane), 1), 1.0, 0.0).astype(BF16)
        every = jnp.sum(tables[...].astype(F32), axis=0).astype(BF16)
        spot = dot(repeat, every[0:n_plane])
        chosen = (spot == (row % ROOM + 1).astype(F32)) & (
            row // ROOM % inner == lane // rows_here
        )
        pick[0] = jnp.where(chosen, 1.0, 0.0).astype(BF16)
        for part in (1, 2):
            wide = dot(repeat, every[part * n_plane : (part + 1) * n_plane])
            pick[part] = jnp.where(chosen, wide, 0.0).astype(BF16)

    def choose_both():
        arrived_tx()
        arrived_ty()
        choose(tables_x, pick_x, lambda k: me_x * n_exp + k, n_head)
        choose(
            tables_y,
            pick_y,
            lambda k: k // CORES * n_exp + me_y * CORES + k % CORES,
            n_y,
        )

    chain = jnp.zeros((near_rows, STATE), F32)
    if n_far > 1:
        put(0, *packed(part, part_log))
        for d in sorted(OWN, reverse=True):
            far_sends.append((member(OWN[d]), far_copy(d, 0, me_far, d)))
            pl.when(far_sends[-1][0])(far_sends[-1][1].start)
    choose_both()
    if n_far > 1:
        for k, group in enumerate(LANDS):
            pl.when(member(group))(far_copy(0, 0, k, 0).wait_recv)
            values, log_here = unpacked(recv_f, k)
            chain = jnp.where(member(group), jnp.exp(log_here) * chain + values, chain)
            if k == RELAY[1]:
                put(2, chain, final)
                far_sends.append((me_far == RELAY[0], far_copy(-1, 2, k, 0)))
                pl.when(far_sends[-1][0])(far_sends[-1][1].start)
        put(1, jnp.exp(part_log) * chain + part, final)
        for d in sorted(UPTO, reverse=True):
            far_sends.append((member(UPTO[d]), far_copy(d, 1, me_far, n_far + d)))
            pl.when(far_sends[-1][0])(far_sends[-1][1].start)

    for k in range(NEAR):
        send_m[k] = (jnp.exp(lpn_ref[k, 0:1, :]) * chain + pn_ref[k]).astype(BF16)
    start_m()
    recv_m[me_near] = send_m[me_near]
    arrived_m()
    chain_in = recv_m[...].astype(F32).reshape(own_rows, STATE)
    for k in range(n_exp):
        send_b[k] = (jnp.exp(lpre_ref[k]) * chain_in + pre_ref[k]).astype(BF16)
    start_b()
    recv_b[me_e] = send_b[me_e]
    arrived_b()

    before = recv_b[...].reshape(channels, STATE)
    normed = []
    for g in range(groups):
        lanes = slice(g * width, (g + 1) * width)
        carried = dot(c_ref[:, g * STATE : (g + 1) * STATE], before[lanes], 1, 1)
        ssm_out = y_ref[:, lanes] + grow_ref[:, lanes] * carried
        z_here = z_ref[:, lanes].astype(F32)
        gated = ssm_out * (z_here / (1.0 + jnp.exp(-z_here)))
        inverse = lax.rsqrt(jnp.mean(gated * gated, axis=1, keepdims=True) + 1e-05)
        normed.append((gated * inverse * normw_ref[:, lanes]).astype(BF16))
    normed = jnp.concatenate(normed, axis=1)
    w_copies[0].wait()
    projected = dot(normed, wout[...], 1, 1).astype(BF16)
    for k in range(n_head):
        send_r[k] = projected[k * rows_here : (k + 1) * rows_here]
    start_r()
    recv_r[me_x] = send_r[me_x]
    arrived_r()
    mixed = jnp.sum(recv_r[...].astype(F32), axis=0)
    hidden = (resid_ref[0].astype(F32) + mixed).astype(BF16).astype(F32)
    scale = lax.rsqrt(jnp.mean(hidden * hidden, axis=1, keepdims=True) + 1e-05)
    moe_in = (hidden * scale * gain_ref[...].reshape(1, -1)).astype(BF16)

    model = moe_in.shape[1]
    split = half_x.shape[1]
    half_x[...] = moe_in[:, :split]
    half_y[...] = moe_in[:, split:]
    start_gx()
    start_gy()
    gathered_x[me_x] = half_x[...]
    gathered_y[me_y] = half_y[...]
    arrived_gx()
    picked = dot(pick_x[0], gathered_x[...].reshape(n_head * rows_here, split))
    rows_x[...] = picked.astype(BF16).reshape(rows_x.shape)
    start_lx()
    arrived_gy()
    picked = dot(pick_y[0], gathered_y[...].reshape(n_y * rows_here, model - split))
    rows_y[...] = picked.astype(BF16).reshape(rows_y.shape)
    start_ly()
    landed_x[me_e] = rows_x[me_e]
    landed_y[:, me_c, me_x] = rows_y[me_block]
    w_copies[1].wait()
    w_copies[2].wait()
    slots = n_plane * ROOM
    arrived_lx()
    raised = dot(landed_x[...].reshape(slots, split), wup[0, :, :split], 1, 1)
    arrived_ly()
    raised += dot(landed_y[...].reshape(slots, model - split), wup[0, :, split:], 1, 1)
    raised = jnp.maximum(raised, 0.0)
    activated = (raised * raised).astype(BF16)

    made_x[...] = dot(activated, wdown[0, :, :split]).astype(BF16).reshape(made_x.shape)
    start_bx()
    made_y[...] = dot(activated, wdown[0, :, split:]).astype(BF16).reshape(made_y.shape)
    start_by()
    back_x[me_e] = made_x[me_e]
    back_y[me_block] = made_y[:, me_c, me_x]
    arrived_bx()
    back = back_x[...].reshape(slots, split)
    summed = dot(pick_x[1], back, 0, 0) + dot(pick_x[2], back, 0, 0)
    sums_x[...] = summed.astype(BF16).reshape(sums_x.shape)
    start_fx()
    arrived_by()
    back = back_y[...].reshape(slots, model - split)
    summed = dot(pick_y[1], back, 0, 0) + dot(pick_y[2], back, 0, 0)
    sums_y[...] = summed.astype(BF16).reshape(sums_y.shape)
    start_fy()
    last_x[me_x] = sums_x[me_x]
    last_y[me_y] = sums_y[me_y]
    arrived_fx()
    moe_sum = jnp.sum(last_x[...].astype(F32), axis=0)
    out_ref[0, :, :split] = (hidden[:, :split] + moe_sum).astype(BF16)
    arrived_fy()
    moe_sum = jnp.sum(last_y[...].astype(F32), axis=0)
    out_ref[0, :, split:] = (hidden[:, split:] + moe_sum).astype(BF16)

    for sent in (sent_a, sent_tx, sent_ty, sent_n, sent_m, sent_b, sent_r):
        sent()
    for sent in (sent_gx, sent_gy, sent_lx, sent_ly, sent_bx, sent_by, sent_fx, sent_fy):
        sent()

    for went, copy in far_sends:
        pl.when(went)(copy.wait_send)


def per_device(
    sizes,
    x_in,
    z_in,
    b_in,
    c_in,
    dt_in,
    a_log,
    d_skip,
    norm_w,
    w_out,
    resid,
    routes,
    gates,
    moe_gain,
    w_up,
    w_down,
):
    n_seq, n_head, n_exp = sizes
    n_far, n_plane = n_seq // NEAR, n_head * n_exp
    tokens, heads = dt_in.shape
    channels = heads * HEAD_DIM
    own_rows = channels // n_exp
    near_rows = own_rows // NEAR
    rows_here, model = resid.shape[1:]
    dma = pltpu.SemaphoreType.DMA
    vmem = pl.BlockSpec(memory_space=pltpu.VMEM)
    hbm = pl.BlockSpec(memory_space=pl.ANY)
    w_out_t = w_out.T
    w_up_t = w_up.transpose(0, 2, 1)
    scratch = [
        pltpu.VMEM(w_out_t.shape, BF16),
        pltpu.VMEM(w_up_t.shape, BF16),
        pltpu.VMEM(w_down.shape, BF16),
        dma((3,)),
        pltpu.VMEM((tokens, channels), F32),
        pltpu.VMEM((tokens, channels), F32),
        pltpu.VMEM((n_exp, own_rows, STATE), F32),
        pltpu.VMEM((n_exp, own_rows, STATE), F32),
    ]

    def pair(count, *block):
        return [
            pltpu.VMEM((count, *block), BF16),
            pltpu.VMEM((count, *block), BF16),
            dma((count,)),
            dma((count,)),
        ]

    scratch += pair(n_exp, own_rows + 16, STATE)
    scratch += pair(NEAR, near_rows + 16, STATE)
    scratch += [
        pltpu.VMEM((NEAR, near_rows, STATE), F32),
        pltpu.VMEM((NEAR, 8, STATE), F32),
        pltpu.VMEM((3, near_rows + 16, STATE), BF16),
        pltpu.VMEM((n_far, near_rows + 16, STATE), BF16),
        dma((2 * n_far,)),
        dma((n_far,)),
    ]
    scratch += pair(NEAR, near_rows, STATE)
    scratch += pair(n_exp, own_rows, STATE)
    scratch += pair(n_head, rows_here, model)
    n_y = n_exp // CORES
    split = model // 256 * 128
    rest = model - split
    slots = n_plane * ROOM

    def crossing(source, landing, count):
        return [pltpu.VMEM(source, BF16), pltpu.VMEM(landing, BF16), dma((count,)), dma((count,))]

    table = (3 * n_plane, n_head * rows_here)
    scratch += crossing(table, (n_head, *table), n_head)
    table = (3 * n_plane, n_y * rows_here)
    scratch += crossing(table, (n_y, *table), n_y)
    scratch += [
        pltpu.VMEM((3, slots, n_head * rows_here), BF16),
        pltpu.VMEM((3, slots, n_y * rows_here), BF16),
    ]
    scratch += crossing((rows_here, split), (n_head, rows_here, split), n_head)
    scratch += crossing((rows_here, rest), (n_y, rows_here, rest), n_y)
    by_exp = (n_exp, n_head, ROOM, split)
    by_block = (n_head * CORES, n_y, ROOM, rest)
    by_source = (n_y, CORES, n_head, ROOM, rest)
    scratch += crossing(by_exp, by_exp, n_exp)
    scratch += crossing(by_block, by_source, n_head * CORES)
    scratch += crossing(by_exp, by_exp, n_exp)
    scratch += crossing(by_source, by_block, n_head * CORES)
    scratch += pair(n_head, rows_here, split)
    scratch += pair(n_y, rows_here, rest)
    return pl.pallas_call(
        functools.partial(kernel, sizes),
        out_shape=jax.ShapeDtypeStruct(resid.shape, BF16),
        in_specs=[vmem] * 12 + [hbm] * 3,
        out_specs=vmem,
        scratch_shapes=scratch,
        compiler_params=pltpu.CompilerParams(
            collective_id=0, has_side_effects=True, vmem_limit_bytes=60 * 2**20
        ),
    )(
        x_in,
        z_in,
        b_in,
        c_in,
        dt_in.T,
        a_log.reshape(1, heads),
        d_skip.reshape(1, heads),
        norm_w.reshape(1, channels),
        resid,
        routes.transpose(2, 0, 1),
        gates.transpose(2, 0, 1),
        moe_gain,
        w_out_t,
        w_up_t,
        w_down,
    )


def solution(mesh):
    sizes = (mesh.shape["seq"], mesh.shape["head"], mesh.shape["exp"])
    placed = (
        P(("seq", "exp"), "head"),
        P(("seq", "exp"), "head"),
        P(("seq", "exp"), "head"),
        P(("seq", "exp"), "head"),
        P(("seq", "exp"), "head"),
        P("head"),
        P("head"),
        P("head"),
        P("head", None),
        P(("seq", "exp"), "head", None),
        P(("seq", "exp"), "head", None),
        P(("seq", "exp"), "head", None),
        P(),
        P(("head", "exp"), None, None),
        P(("head", "exp"), None, None),
    )
    return jax.shard_map(
        functools.partial(per_device, sizes),
        mesh=mesh,
        in_specs=placed,
        out_specs=P(("seq", "exp"), "head", None),
        check_vma=False,
    )
```

```python
import functools

import jax
import jax.numpy as jnp
from jax import lax
from jax.experimental import pallas as pl
from jax.experimental.pallas import tpu as pltpu
from jax.sharding import PartitionSpec as P

HEAD_DIM = 64
STATE = 128
ROOM = 16
CORES = 2
NEAR = 4
OWN = {1: (0, 2, 3, 4, 5, 6), 2: (4, 5), 3: (4,)}
UPTO = {1: (1, 3), 2: (1,), 6: (1,)}
RELAY = (7, 1, (-1, -2))
LANDS = ((1,), (2, 3, 5, 6, 7), (3,), (4,), (5, 6, 7), (6, 7), (7,))
RUN = 7
F32 = jnp.float32
BF16 = jnp.bfloat16
MESH = pl.DeviceIdType.MESH
EXACT = lax.Precision.HIGHEST


def dot(a, b, ca=1, cb=0, precision=None):
    return lax.dot_general(
        a, b, (((ca,), (cb,)), ((), ())), preferred_element_type=F32, precision=precision
    )


def iota(shape, dim):
    return lax.broadcasted_iota(jnp.int32, shape, dim)


def halves(values):
    high = values.astype(BF16)
    low = (values - high.astype(F32)).astype(BF16)
    return high, low


def kernel(
    sizes,
    x_ref,
    z_ref,
    b_ref,
    c_ref,
    dt_ref,
    alog_ref,
    dskip_ref,
    normw_ref,
    resid_ref,
    routes_ref,
    gates_ref,
    gain_ref,
    wout_hbm,
    wup_hbm,
    wdown_hbm,
    out_ref,
    wout,
    wup,
    wdown,
    wsem,
    y_ref,
    grow_ref,
    pre_ref,
    lpre_ref,
    send_a,
    recv_a,
    sa_sem,
    ra_sem,
    send_n,
    recv_n,
    sn_sem,
    rn_sem,
    pn_ref,
    lpn_ref,
    send_f,
    recv_f,
    sf_sem,
    rf_sem,
    send_m,
    recv_m,
    sm_sem,
    rm_sem,
    send_b,
    recv_b,
    sb_sem,
    rb_sem,
    send_r,
    recv_r,
    sr_sem,
    rr_sem,
    send_q,
    recv_q,
    sq_sem,
    rq_sem,
    table_x,
    tables_x,
    tx_send,
    tx_recv,
    table_y,
    tables_y,
    ty_send,
    ty_recv,
    pick_x,
    pick_y,
    gates_x,
    gates_y,
    half_x,
    gathered_x,
    gx_send,
    gx_recv,
    half_y,
    gathered_y,
    gy_send,
    gy_recv,
    rows_x,
    landed_x,
    lx_send,
    lx_recv,
    rows_y,
    landed_y,
    ly_send,
    ly_recv,
    made_x,
    back_x,
    bx_send,
    bx_recv,
    made_y,
    back_y,
    by_send,
    by_recv,
    sums_x,
    last_x,
    fx_send,
    fx_recv,
    sums_y,
    last_y,
    fy_send,
    fy_recv,
):
    n_seq, n_head, n_exp = sizes
    n_far = n_seq // NEAR
    n_plane = n_head * n_exp
    tokens = x_ref.shape[0]
    heads = dt_ref.shape[0]
    groups = b_ref.shape[1] // STATE
    per_group = heads // groups
    width = per_group * HEAD_DIM
    own_heads = heads // n_exp
    own_rows = own_heads * HEAD_DIM
    near_rows = own_rows // NEAR
    rows_here = resid_ref.shape[1]

    me_z = lax.axis_index("seq")
    me_x = lax.axis_index("head")
    me_e = lax.axis_index("exp")
    me_far = me_z // NEAR
    me_near = me_z % NEAR
    n_y = n_exp // CORES
    me_y = me_e // CORES
    me_c = me_e % CORES
    me_block = me_x * CORES + me_c

    w_copies = [
        pltpu.make_async_copy(wout_hbm, wout, wsem.at[0]),
        pltpu.make_async_copy(wup_hbm, wup, wsem.at[1]),
        pltpu.make_async_copy(wdown_hbm, wdown, wsem.at[2]),
    ]
    for copy in w_copies:
        copy.start()

    def exp_id(d):
        there = lax.rem(me_e + d, n_exp)
        return there, {"exp": there}

    def head_id(d):
        there = lax.rem(me_x + d, n_head)
        return there, {"head": there}

    def y_id(d):
        there = lax.rem(me_y + d, n_y)
        return there, {"exp": there * CORES + me_c}

    def block_id(d):
        there = lax.rem(me_block + d, n_head * CORES)
        return there, {"head": there // CORES, "exp": me_y * CORES + there % CORES}

    def near_id(d):
        there = lax.rem(me_near + d, NEAR)
        return there, {"seq": me_far * NEAR + there}

    def far_id(d):
        return {"seq": (me_far + d) * NEAR + me_near}

    barrier = pltpu.get_barrier_semaphore()

    def greet(peer, count):
        def one(d, carry):
            pl.semaphore_signal(barrier, inc=1, device_id=peer(d)[1], device_id_type=MESH)
            return carry

        lax.fori_loop(1, count, one, 0)

    def member(set_of):
        found = me_far < 0
        for group in set_of:
            found = found | (me_far == group)
        return found

    def greet_far(d):
        pl.semaphore_signal(barrier, inc=1, device_id=far_id(d), device_id_type=MESH)

    far_peers = 0
    if n_far > 1:
        assert n_far == len(LANDS) + 1
        for d in range(1, n_far):
            low = set(OWN.get(d, ())) | set(UPTO.get(d, ()))
            for there, ends in ((d, low), (-d, {group + d for group in low})):
                if ends:
                    meets = member(sorted(ends))
                    pl.when(meets)(functools.partial(greet_far, there))
                    far_peers = far_peers + jnp.where(meets, 1, 0)
    greet(near_id, NEAR)
    greet(exp_id, n_exp)
    for d in range(1, n_head):
        for core in range(CORES):
            where = {"head": lax.rem(me_x + d, n_head), "exp": me_y * CORES + core}
            pl.semaphore_signal(barrier, inc=1, device_id=where, device_id_type=MESH)

    def exchange(peer, count, source, landing, mine, send_sems, recv_sems):
        def copy(there, where, place):
            return pltpu.make_async_remote_copy(
                src_ref=source(there),
                dst_ref=landing(place),
                send_sem=send_sems.at[there],
                recv_sem=recv_sems.at[place],
                device_id=where,
                device_id_type=MESH,
            )

        def start(k, carry):
            there, where = peer(1 + lax.rem(k + count // 2 - 2, count - 1))
            copy(there, where, mine).start()
            return carry

        def sent(d, carry):
            there, where = peer(d)
            copy(there, where, mine).wait_send()
            return carry

        def arrived(d, carry):
            there, where = peer(d)
            copy(there, where, there).wait_recv()
            return carry

        return (
            lambda: lax.fori_loop(1, count, start, 0),
            lambda: lax.fori_loop(1, count, arrived, 0),
            lambda: lax.fori_loop(1, count, sent, 0),
        )

    def at(ref):
        return lambda k: ref.at[k]

    def whole(ref):
        return lambda k: ref

    def across(ref):
        return lambda k: ref.at[:, k % CORES, k // CORES]

    start_a, arrived_a, sent_a = exchange(
        exp_id, n_exp, at(send_a), at(recv_a), me_e, sa_sem, ra_sem
    )
    start_n, arrived_n, sent_n = exchange(
        near_id, NEAR, at(send_n), at(recv_n), me_near, sn_sem, rn_sem
    )
    start_m, arrived_m, sent_m = exchange(
        near_id, NEAR, at(send_m), at(recv_m), me_near, sm_sem, rm_sem
    )
    start_b, arrived_b, sent_b = exchange(
        exp_id, n_exp, at(send_b), at(recv_b), me_e, sb_sem, rb_sem
    )
    start_r, arrived_r, sent_r = exchange(
        head_id, n_head, at(send_r), at(recv_r), me_x, sr_sem, rr_sem
    )
    start_q, arrived_q, sent_q = exchange(
        head_id, n_head, at(send_q), at(recv_q), me_x, sq_sem, rq_sem
    )
    start_tx, arrived_tx, sent_tx = exchange(
        head_id, n_head, whole(table_x), at(tables_x), me_x, tx_send, tx_recv
    )
    start_ty, arrived_ty, sent_ty = exchange(
        y_id, n_y, whole(table_y), at(tables_y), me_y, ty_send, ty_recv
    )
    start_gx, arrived_gx, sent_gx = exchange(
        head_id, n_head, whole(half_x), at(gathered_x), me_x, gx_send, gx_recv
    )
    start_gy, arrived_gy, sent_gy = exchange(
        y_id, n_y, whole(half_y), at(gathered_y), me_y, gy_send, gy_recv
    )
    start_lx, arrived_lx, sent_lx = exchange(
        exp_id, n_exp, at(rows_x), at(landed_x), me_e, lx_send, lx_recv
    )
    start_ly, arrived_ly, sent_ly = exchange(
        block_id, n_head * CORES, at(rows_y), across(landed_y), me_block, ly_send, ly_recv
    )
    start_bx, arrived_bx, sent_bx = exchange(
        exp_id, n_exp, at(made_x), at(back_x), me_e, bx_send, bx_recv
    )
    start_by, arrived_by, sent_by = exchange(
        block_id, n_head * CORES, across(made_y), at(back_y), me_block, by_send, by_recv
    )
    start_fx, arrived_fx, sent_fx = exchange(
        head_id, n_head, at(sums_x), at(last_x), me_x, fx_send, fx_recv
    )
    start_fy, arrived_fy, sent_fy = exchange(
        y_id, n_y, at(sums_y), at(last_y), me_y, fy_send, fy_recv
    )

    dt = dt_ref[...]
    step_t = jnp.maximum(dt, 0.0) + jnp.log1p(jnp.exp(-jnp.abs(dt)))
    decay_rate = jnp.broadcast_to(jnp.exp(alog_ref[...]), (heads, heads))
    same_head = iota((heads, heads), 0) == iota((heads, heads), 1)
    decay_rate = jnp.sum(jnp.where(same_head, decay_rate, 0.0), axis=1, keepdims=True)
    rate_t = -step_t * decay_rate
    row_t, col_t = iota((tokens, tokens), 0), iota((tokens, tokens), 1)
    causal = row_t >= col_t
    upto = jnp.where(causal, 1.0, 0.0)
    cum_t = dot(rate_t, upto, 1, 1, EXACT)
    cum = dot(upto, rate_t, 1, 1, EXACT)
    step = dot(jnp.where(row_t == col_t, 1.0, 0.0), step_t, 1, 1, EXACT)
    tail = jnp.exp(cum[tokens - 1 : tokens, :] - cum) * step
    grow = jnp.exp(cum)
    channels = heads * HEAD_DIM
    spread = jnp.where(
        iota((heads, channels), 1) // HEAD_DIM == iota((heads, channels), 0), 1.0, 0.0
    )
    tail_wide = dot(tail, spread, 1, 0, EXACT)
    weighted = (tail_wide * x_ref[...].astype(F32)).astype(BF16)

    total = jnp.broadcast_to(cum_t[:, tokens - 1 : tokens], (heads, STATE))
    total_high, total_low = halves(total)
    per_send = n_exp // groups
    for g in range(groups):
        update = dot(
            weighted[:, g * width : (g + 1) * width],
            b_ref[:, g * STATE : (g + 1) * STATE],
            0,
            0,
        ).astype(BF16)
        for k in range(per_send):
            send_a[g * per_send + k, 0:own_rows, :] = update[k * own_rows : (k + 1) * own_rows, :]
    tile_row = iota((n_exp * 16, 2 * heads), 0)
    its_head = tile_row // 16 * own_heads + tile_row % own_heads + heads * (tile_row % 16 // 8)
    logs = dot(
        jnp.where(its_head == iota((n_exp * 16, 2 * heads), 1), 1.0, 0.0).astype(BF16),
        jnp.concatenate([total_high, total_low], axis=0),
    ).astype(BF16)
    for k in range(n_exp):
        send_a[k, own_rows : own_rows + 16, :] = logs[k * 16 : (k + 1) * 16]

    pl.semaphore_wait(barrier, far_peers + (NEAR - 1) + (n_exp - 1) + (n_head - 1) * CORES)
    start_a()
    recv_a[me_e] = send_a[me_e]

    expert_row = iota((n_plane, rows_here), 0)
    routed = jnp.zeros((n_plane, rows_here), F32)
    gate = jnp.zeros((n_plane, rows_here), F32)
    for k in range(routes_ref.shape[0]):
        hit = expert_row == routes_ref[k]
        routed = jnp.where(hit, 1.0, routed)
        gate = jnp.where(hit, gates_ref[k], gate)
    upto_here = jnp.where(
        iota((rows_here, rows_here), 0) <= iota((rows_here, rows_here), 1), 1.0, 0.0
    ).astype(BF16)
    place = routed * dot(routed.astype(BF16), upto_here)
    gate_high, gate_low = halves(gate)
    table = jnp.concatenate([place.astype(BF16), gate_high, gate_low], axis=0)

    def in_lanes(count, mine):
        lanes = (rows_here, count * rows_here)
        spot = iota(lanes, 1) == iota(lanes, 0) + mine * rows_here
        return dot(table, jnp.where(spot, 1.0, 0.0).astype(BF16)).astype(BF16)

    table_x[...] = in_lanes(n_head, me_x)
    table_y[...] = in_lanes(n_y, me_y)
    start_tx()
    start_ty()
    tables_x[me_x] = table_x[...]
    tables_y[me_y] = table_y[...]

    first_half = iota((tokens, 2 * HEAD_DIM), 1) < HEAD_DIM
    skip_wide = dot(dskip_ref[...], spread, 1, 0, EXACT)
    for g in range(groups):
        scores = dot(
            c_ref[:, g * STATE : (g + 1) * STATE], b_ref[:, g * STATE : (g + 1) * STATE], 1, 1
        )
        for j in range(g * per_group // 2, (g + 1) * per_group // 2):
            lanes = slice(2 * HEAD_DIM * j, 2 * HEAD_DIM * (j + 1))
            mixes = []
            for h in (2 * j, 2 * j + 1):
                distance = cum[:, h : h + 1] - cum_t[h : h + 1, :]
                decay = jnp.where(causal, jnp.exp(jnp.where(causal, distance, 0.0)), 0.0)
                mixes.append((scores * (decay * step_t[h : h + 1, :])).astype(BF16))
            pair = x_ref[:, lanes]
            zero = jnp.zeros_like(pair)
            stacked = jnp.concatenate(
                [jnp.where(first_half, pair, zero), jnp.where(first_half, zero, pair)], axis=0
            )
            inside = dot(jnp.concatenate(mixes, axis=1), stacked)
            y_ref[:, lanes] = inside + skip_wide[:, lanes] * pair.astype(F32)
    grow_ref[...] = dot(grow, spread, 1, 0, EXACT)

    arrived_a()
    own_row = iota((own_rows, STATE), 0)
    state = jnp.zeros((own_rows, STATE), F32)
    log_sum = jnp.zeros((own_rows, STATE), F32)
    for k in range(n_exp):
        pre_ref[k] = state
        lpre_ref[k] = log_sum
        tile = recv_a[k, own_rows : own_rows + 16, :].astype(F32)
        log_here = jnp.zeros((own_rows, STATE), F32)
        for h in range(own_heads):
            one = tile[h : h + 1, :] + tile[8 + h : 9 + h, :]
            log_here = jnp.where(own_row // HEAD_DIM == h, one, log_here)
        state = jnp.exp(log_here) * state + recv_a[k, 0:own_rows, :].astype(F32)
        log_sum = log_sum + log_here

    def packed(values, logs):
        high, low = halves(logs)
        tile = jnp.where(
            iota((16, STATE), 0) < 8,
            jnp.broadcast_to(high.astype(F32), (16, STATE)),
            jnp.broadcast_to(low.astype(F32), (16, STATE)),
        )
        return values.astype(BF16), tile.astype(BF16)

    def unpacked(ref, k):
        tile = ref[k, near_rows : near_rows + 16, :].astype(F32)
        return ref[k, 0:near_rows, :].astype(F32), tile[0:1, :] + tile[8:9, :]

    for k in range(NEAR):
        rows = slice(k * near_rows, (k + 1) * near_rows)
        values, tile = packed(state[rows], log_sum[k * near_rows : k * near_rows + 1])
        send_n[k, 0:near_rows, :] = values
        send_n[k, near_rows : near_rows + 16, :] = tile
    start_n()
    recv_n[me_near] = send_n[me_near]
    arrived_n()
    part = jnp.zeros((near_rows, STATE), F32)
    part_log = jnp.zeros((1, STATE), F32)
    for k in range(NEAR):
        pn_ref[k] = part
        lpn_ref[k] = jnp.broadcast_to(part_log, (8, STATE))
        values, log_here = unpacked(recv_n, k)
        part = jnp.exp(log_here) * part + values
        part_log = part_log + log_here
    def far_copy(d, source, slot, sem):
        return pltpu.make_async_remote_copy(
            src_ref=send_f.at[source],
            dst_ref=recv_f.at[slot],
            send_sem=sf_sem.at[sem],
            recv_sem=rf_sem.at[slot],
            device_id=far_id(d),
            device_id_type=MESH,
        )

    def put(slot, values, tile):
        send_f[slot, 0:near_rows, :] = values.astype(BF16)
        send_f[slot, near_rows : near_rows + 16, :] = tile

    final = jnp.full((16, STATE), -16384.0, BF16)
    far_sends = []

    def choose(tables, pick, gate_pick, expert, inner):
        row, lane = iota(pick.shape, 0), iota(pick.shape, 1)
        slots = pick.shape[0]
        wanted = expert(iota((slots, n_plane), 0) // (inner * ROOM))
        repeat = jnp.where(wanted == iota((slots, n_plane), 1), 1.0, 0.0).astype(BF16)
        every = jnp.sum(tables[...].astype(F32), axis=0).astype(BF16)
        spot = dot(repeat, every[0:n_plane])
        chosen = (spot == (row % ROOM + 1).astype(F32)) & (
            row // ROOM % inner == lane // rows_here
        )
        pick[...] = jnp.where(chosen, 1.0, 0.0).astype(BF16)
        for part in (1, 2):
            wide = dot(repeat, every[part * n_plane : (part + 1) * n_plane])
            gate_pick[part - 1] = jnp.where(chosen, wide, 0.0).T.astype(BF16)

    def choose_both():
        arrived_tx()
        arrived_ty()
        choose(tables_x, pick_x, gates_x, lambda k: me_x * n_exp + k, n_head)
        choose(
            tables_y,
            pick_y,
            gates_y,
            lambda k: k // CORES * n_exp + me_y * CORES + k % CORES,
            n_y,
        )

    chain = jnp.zeros((near_rows, STATE), F32)
    if n_far > 1:
        for group, slot in ((3, 2), (4, RUN)):
            pl.when(me_far == group)(far_copy(0, 0, slot, 0).wait_recv)
        run, run_log = part, part_log
        for group, slot in ((3, 2), (4, RUN)):
            values, log_here = unpacked(recv_f, slot)
            run = jnp.where(me_far == group, jnp.exp(part_log) * values + part, run)
            run_log = jnp.where(me_far == group, log_here + part_log, run_log)
        put(0, *packed(run, run_log))
        for d in sorted(OWN, reverse=True):
            slot = jnp.where(me_far == 3, RUN, me_far)
            far_sends.append((member(OWN[d]), far_copy(d, 0, slot, d)))
            pl.when(far_sends[-1][0])(far_sends[-1][1].start)
    choose_both()
    if n_far > 1:
        for k, group in enumerate(LANDS):
            if k != 2:
                pl.when(member(group))(far_copy(0, 0, k, 0).wait_recv)
            values, log_here = unpacked(recv_f, k)
            chain = jnp.where(member(group), jnp.exp(log_here) * chain + values, chain)
            if k == RELAY[1]:
                put(2, chain, final)
                for sem, d in zip((0, n_far - 1), RELAY[2]):
                    far_sends.append((me_far == RELAY[0], far_copy(d, 2, k, sem)))
                    pl.when(far_sends[-1][0])(far_sends[-1][1].start)
        put(1, jnp.exp(part_log) * chain + part, final)
        for d in sorted(UPTO, reverse=True):
            far_sends.append((member(UPTO[d]), far_copy(d, 1, me_far, n_far + d)))
            pl.when(far_sends[-1][0])(far_sends[-1][1].start)

    for k in range(NEAR):
        send_m[k] = (jnp.exp(lpn_ref[k, 0:1, :]) * chain + pn_ref[k]).astype(BF16)
    start_m()
    recv_m[me_near] = send_m[me_near]
    arrived_m()
    chain_in = recv_m[...].astype(F32).reshape(own_rows, STATE)
    for k in range(n_exp):
        send_b[k] = (jnp.exp(lpre_ref[k]) * chain_in + pre_ref[k]).astype(BF16)
    start_b()
    recv_b[me_e] = send_b[me_e]
    arrived_b()

    before = recv_b[...].reshape(channels, STATE)
    normed = []
    for g in range(groups):
        lanes = slice(g * width, (g + 1) * width)
        carried = dot(c_ref[:, g * STATE : (g + 1) * STATE], before[lanes], 1, 1)
        ssm_out = y_ref[:, lanes] + grow_ref[:, lanes] * carried
        z_here = z_ref[:, lanes].astype(F32)
        gated = ssm_out * (z_here / (1.0 + jnp.exp(-z_here)))
        inverse = lax.rsqrt(jnp.mean(gated * gated, axis=1, keepdims=True) + 1e-05)
        normed.append((gated * inverse * normw_ref[:, lanes]).astype(BF16))
    normed = jnp.concatenate(normed, axis=1)
    w_copies[0].wait()
    split = half_x.shape[1]
    for send, rows, start in ((send_r, wout[:split], start_r), (send_q, wout[split:], start_q)):
        projected = dot(normed, rows, 1, 1).astype(BF16)
        for k in range(n_head):
            send[k] = projected[k * rows_here : (k + 1) * rows_here]
        start()
    recv_r[me_x] = send_r[me_x]
    recv_q[me_x] = send_q[me_x]
    arrived_r()
    mixed = jnp.sum(recv_r[...].astype(F32), axis=0)
    arrived_q()
    mixed = jnp.concatenate([mixed, jnp.sum(recv_q[...].astype(F32), axis=0)], axis=1)
    hidden = (resid_ref[0].astype(F32) + mixed).astype(BF16).astype(F32)
    scale = lax.rsqrt(jnp.mean(hidden * hidden, axis=1, keepdims=True) + 1e-05)
    moe_in = (hidden * scale * gain_ref[...].reshape(1, -1)).astype(BF16)

    model = moe_in.shape[1]
    half_x[...] = moe_in[:, :split]
    half_y[...] = moe_in[:, split:]
    start_gx()
    start_gy()
    gathered_x[me_x] = half_x[...]
    gathered_y[me_y] = half_y[...]
    arrived_gx()
    picked = dot(pick_x[...], gathered_x[...].reshape(n_head * rows_here, split))
    rows_x[...] = picked.astype(BF16).reshape(rows_x.shape)
    start_lx()
    arrived_gy()
    picked = dot(pick_y[...], gathered_y[...].reshape(n_y * rows_here, model - split))
    rows_y[...] = picked.astype(BF16).reshape(rows_y.shape)
    start_ly()
    landed_x[me_e] = rows_x[me_e]
    landed_y[:, me_c, me_x] = rows_y[me_block]
    w_copies[1].wait()
    w_copies[2].wait()
    slots = n_plane * ROOM
    arrived_lx()
    raised = dot(landed_x[...].reshape(slots, split), wup[0, :, :split], 1, 1)
    arrived_ly()
    raised += dot(landed_y[...].reshape(slots, model - split), wup[0, :, split:], 1, 1)
    raised = jnp.maximum(raised, 0.0)
    activated = (raised * raised).astype(BF16)

    made_x[...] = dot(activated, wdown[0, :, :split]).astype(BF16).reshape(made_x.shape)
    start_bx()
    made_y[...] = dot(activated, wdown[0, :, split:]).astype(BF16).reshape(made_y.shape)
    start_by()
    back_x[me_e] = made_x[me_e]
    back_y[me_block] = made_y[:, me_c, me_x]
    arrived_bx()
    back = back_x[...].reshape(slots, split)
    summed = dot(gates_x[0], back) + dot(gates_x[1], back)
    sums_x[...] = summed.astype(BF16).reshape(sums_x.shape)
    start_fx()
    arrived_by()
    back = back_y[...].reshape(slots, model - split)
    summed = dot(gates_y[0], back) + dot(gates_y[1], back)
    sums_y[...] = summed.astype(BF16).reshape(sums_y.shape)
    start_fy()
    last_x[me_x] = sums_x[me_x]
    last_y[me_y] = sums_y[me_y]
    arrived_fx()
    moe_sum = jnp.sum(last_x[...].astype(F32), axis=0)
    out_ref[0, :, :split] = (hidden[:, :split] + moe_sum).astype(BF16)
    arrived_fy()
    moe_sum = jnp.sum(last_y[...].astype(F32), axis=0)
    out_ref[0, :, split:] = (hidden[:, split:] + moe_sum).astype(BF16)

    for sent in (sent_a, sent_tx, sent_ty, sent_n, sent_m, sent_b, sent_r, sent_q):
        sent()
    for sent in (sent_gx, sent_gy, sent_lx, sent_ly, sent_bx, sent_by, sent_fx, sent_fy):
        sent()

    for went, copy in far_sends:
        pl.when(went)(copy.wait_send)


def per_device(
    sizes,
    x_in,
    z_in,
    b_in,
    c_in,
    dt_in,
    a_log,
    d_skip,
    norm_w,
    w_out,
    resid,
    routes,
    gates,
    moe_gain,
    w_up,
    w_down,
):
    n_seq, n_head, n_exp = sizes
    n_far, n_plane = n_seq // NEAR, n_head * n_exp
    tokens, heads = dt_in.shape
    channels = heads * HEAD_DIM
    own_rows = channels // n_exp
    near_rows = own_rows // NEAR
    rows_here, model = resid.shape[1:]
    dma = pltpu.SemaphoreType.DMA
    vmem = pl.BlockSpec(memory_space=pltpu.VMEM)
    hbm = pl.BlockSpec(memory_space=pl.ANY)
    w_out_t = w_out.T
    w_up_t = w_up.transpose(0, 2, 1)
    scratch = [
        pltpu.VMEM(w_out_t.shape, BF16),
        pltpu.VMEM(w_up_t.shape, BF16),
        pltpu.VMEM(w_down.shape, BF16),
        dma((3,)),
        pltpu.VMEM((tokens, channels), F32),
        pltpu.VMEM((tokens, channels), F32),
        pltpu.VMEM((n_exp, own_rows, STATE), F32),
        pltpu.VMEM((n_exp, own_rows, STATE), F32),
    ]

    def pair(count, *block):
        return [
            pltpu.VMEM((count, *block), BF16),
            pltpu.VMEM((count, *block), BF16),
            dma((count,)),
            dma((count,)),
        ]

    scratch += pair(n_exp, own_rows + 16, STATE)
    scratch += pair(NEAR, near_rows + 16, STATE)
    scratch += [
        pltpu.VMEM((NEAR, near_rows, STATE), F32),
        pltpu.VMEM((NEAR, 8, STATE), F32),
        pltpu.VMEM((3, near_rows + 16, STATE), BF16),
        pltpu.VMEM((n_far, near_rows + 16, STATE), BF16),
        dma((2 * n_far,)),
        dma((n_far,)),
    ]
    scratch += pair(NEAR, near_rows, STATE)
    scratch += pair(n_exp, own_rows, STATE)
    n_y = n_exp // CORES
    split = model // 256 * 128
    rest = model - split
    scratch += pair(n_head, rows_here, split)
    scratch += pair(n_head, rows_here, rest)
    slots = n_plane * ROOM

    def crossing(source, landing, count):
        return [pltpu.VMEM(source, BF16), pltpu.VMEM(landing, BF16), dma((count,)), dma((count,))]

    table = (3 * n_plane, n_head * rows_here)
    scratch += crossing(table, (n_head, *table), n_head)
    table = (3 * n_plane, n_y * rows_here)
    scratch += crossing(table, (n_y, *table), n_y)
    scratch += [
        pltpu.VMEM((slots, n_head * rows_here), BF16),
        pltpu.VMEM((slots, n_y * rows_here), BF16),
        pltpu.VMEM((2, n_head * rows_here, slots), BF16),
        pltpu.VMEM((2, n_y * rows_here, slots), BF16),
    ]
    scratch += crossing((rows_here, split), (n_head, rows_here, split), n_head)
    scratch += crossing((rows_here, rest), (n_y, rows_here, rest), n_y)
    by_exp = (n_exp, n_head, ROOM, split)
    by_block = (n_head * CORES, n_y, ROOM, rest)
    by_source = (n_y, CORES, n_head, ROOM, rest)
    scratch += crossing(by_exp, by_exp, n_exp)
    scratch += crossing(by_block, by_source, n_head * CORES)
    scratch += crossing(by_exp, by_exp, n_exp)
    scratch += crossing(by_source, by_block, n_head * CORES)
    scratch += pair(n_head, rows_here, split)
    scratch += pair(n_y, rows_here, rest)
    return pl.pallas_call(
        functools.partial(kernel, sizes),
        out_shape=jax.ShapeDtypeStruct(resid.shape, BF16),
        in_specs=[vmem] * 12 + [hbm] * 3,
        out_specs=vmem,
        scratch_shapes=scratch,
        compiler_params=pltpu.CompilerParams(
            collective_id=0, has_side_effects=True, vmem_limit_bytes=60 * 2**20
        ),
    )(
        x_in,
        z_in,
        b_in,
        c_in,
        dt_in.T,
        a_log.reshape(1, heads),
        d_skip.reshape(1, heads),
        norm_w.reshape(1, channels),
        resid,
        routes.transpose(2, 0, 1),
        gates.transpose(2, 0, 1),
        moe_gain,
        w_out_t,
        w_up_t,
        w_down,
    )


def solution(mesh):
    sizes = (mesh.shape["seq"], mesh.shape["head"], mesh.shape["exp"])
    placed = (
        P(("seq", "exp"), "head"),
        P(("seq", "exp"), "head"),
        P(("seq", "exp"), "head"),
        P(("seq", "exp"), "head"),
        P(("seq", "exp"), "head"),
        P("head"),
        P("head"),
        P("head"),
        P("head", None),
        P(("seq", "exp"), "head", None),
        P(("seq", "exp"), "head", None),
        P(("seq", "exp"), "head", None),
        P(),
        P(("head", "exp"), None, None),
        P(("head", "exp"), None, None),
    )
    return jax.shard_map(
        functools.partial(per_device, sizes),
        mesh=mesh,
        in_specs=placed,
        out_specs=P(("seq", "exp"), "head", None),
        check_vma=False,
    )
```
